256 devices in a mesh: stream: 64 (over y, z_lo, x, core), strip: 4 (over z_hi).
Axes of the slice: x: 4, y: 4, z: 8 (z_hi: 4, z_lo: 2; z = z_hi * 2 + z_lo), core: 2. Of those that a mesh axis runs over, the one named last changes fastest.
Arguments:
- loader_rows: bfloat16 [64, 512, 48], P('stream', 'strip'), may hold values from -12 to 12
- load_owner: int32 [64, 512], P('stream', 'strip'), may hold values from 0 to 63, as said below
- load_slot: int32 [64, 512], P('stream', 'strip'), may hold values from 0 to 127, as said below
- valid_frames: int32 [64], P('stream'), may hold values from 1 to 8
- next_owner: int32 [64], P('stream'), may hold values from 0 to 63, as said below
- pixel_cache: bfloat16 [64, 2, 64, 48], P('stream', None, 'strip'), may hold values from -6 to 6
- act_cache: bfloat16 [64, 2, 64, 16, 128], P('stream', None, 'strip'), may hold values from -4 to 4
- res_cache: bfloat16 [64, 2, 64, 16, 128], P('stream', None, 'strip'), may hold values from -8 to 8
- stem_weight: bfloat16 [3, 3, 3, 3, 128], replicated, may hold values from -0.625 to 0.625
- norm_gain: float32 [128], replicated, may hold values from 0.1 to 1.9
- norm_bias: float32 [128], replicated, may hold values from -2.5 to 2.5
- conv_weight: bfloat16 [3, 3, 3, 128, 128], replicated, may hold values from -0.109375 to 0.109375
- down_weight: bfloat16 [3, 3, 3, 128, 256], replicated, may hold values from -0.109375 to 0.109375
Outputs:
- latents: bfloat16 [64, 4, 32, 8, 256], P('stream', None, 'strip')
- next_pixel_cache: bfloat16 [64, 2, 64, 48], P('stream', None, 'strip')
- next_act_cache: bfloat16 [64, 2, 64, 16, 128], P('stream', None, 'strip')
- next_res_cache: bfloat16 [64, 2, 64, 16, 128], P('stream', None, 'strip')
The draws below stay inside these ranges and needn't reach their ends.
Inputs may be any that keep to these rules, and one draw needn't show every extreme that they name: `load_owner`: among the 128 positions of one stream that fall in one strip, every stream is named by exactly 2. `load_slot`: over all loader rows of strip j that name the same owner, the slots are all different, so each owner receives every slot of strip j exactly once. `next_owner`: A permutation made by passes over the index bits 0, 1, 2 and so on in this order, each pass exchanging some pairs of indices that differ only in that bit.
All inputs are finite; a program needn't handle non-finite values.
Results may differ from the reference program's by a relative error of at most 0.0055.
Values may be sent and summed in bfloat16 or wider, within the bound.
A program may use at most 64 MiB of HBM per device.

```python
import jax
import jax.numpy as jnp
from jax import lax

FRAMES = 8
R_DEV = 16
COLS = 16
C1 = 128
C2 = 256
GROUPS = 32
STREAMS = 64
ROWS = 64
N_STRIP = 4


def loader_plan(key):
    row_fill = FRAMES * R_DEV
    strip_count = ROWS // R_DEV
    per_peer = row_fill // STREAMS
    repeated = jnp.arange(row_fill, dtype=jnp.int32) // per_peer
    owner_keys = jax.random.split(jax.random.fold_in(key, 11), strip_count * STREAMS)
    owners = jax.vmap(lambda one_key: jax.random.permutation(one_key, repeated))(owner_keys)
    owners = owners.reshape(strip_count, STREAMS, row_fill)
    onehot = (owners[..., None] == jnp.arange(STREAMS, dtype=jnp.int32)).astype(jnp.int32)
    rank_in = jnp.sum(jnp.cumsum(onehot, axis=2) * onehot, axis=3) - 1
    position = jnp.arange(STREAMS, dtype=jnp.int32)[None, :, None] * per_peer + rank_in
    slot_keys = jax.random.split(jax.random.fold_in(key, 12), strip_count * STREAMS)
    tables = jax.vmap(lambda one_key: jax.random.permutation(one_key, row_fill))(slot_keys)
    tables = tables.reshape(strip_count, STREAMS, row_fill)
    strip_ids = jnp.arange(strip_count, dtype=jnp.int32)[:, None, None]
    slots = tables[strip_ids, owners, position]
    owner_out = owners.transpose(1, 0, 2).reshape(STREAMS, strip_count * row_fill)
    slot_out = slots.transpose(1, 0, 2).reshape(STREAMS, strip_count * row_fill)
    return (owner_out.astype(jnp.int32), slot_out.astype(jnp.int32))


def draw_load_owner(key, part):
    return loader_plan(key)[0]


def draw_load_slot(key, part):
    return loader_plan(key)[1]


def draw_loader_rows(key, part):
    owner_out, slot_out = loader_plan(key)
    row_fill = FRAMES * R_DEV
    strip_ids = jnp.arange(FRAMES * ROWS, dtype=jnp.int32) // row_fill
    global_row = (strip_ids[None, :] * R_DEV + slot_out % R_DEV).astype(jnp.int32)
    row_scale = 1.0 + 2.0 * global_row.astype(jnp.float32) / max(ROWS - 1, 1)
    shape_out = (STREAMS, FRAMES * ROWS, 3 * COLS)
    values = jnp.clip(jax.random.normal(jax.random.fold_in(key, 13), shape_out, jnp.float32), -4.0, 4.0)
    return (values * row_scale[..., None]).astype(jnp.bfloat16)


def draw_next_owner(key, part):
    section_count = STREAMS.bit_length() - 1
    position = jnp.arange(STREAMS, dtype=jnp.int32)
    for bit_pos in range(section_count):
        flags = jax.random.randint(jax.random.fold_in(key, 20 + bit_pos), (STREAMS,), 0, 2)
        pair_id = position - position // (1 << bit_pos) % 2 * (1 << bit_pos)
        flipped = flags[pair_id] == 1
        position = jnp.where(flipped, jnp.bitwise_xor(position, 1 << bit_pos), position)
    return position.astype(jnp.int32)


def place_ends(array, key, smallest, high):
    extent = array.shape
    spot = [jax.random.randint(jax.random.fold_in(key, axis), (), 0, extent[axis]) for axis in range(len(extent))]
    array = array.at[tuple(spot)].set(smallest)
    longest = extent.index(max(extent))
    spot[longest] = (spot[longest] + 1) % extent[longest]
    return array.at[tuple(spot)].set(high)


def block_levels(key, extent, shards, smallest, top_value):
    def one(dim, blocks):
        steps = jax.random.uniform(jax.random.fold_in(jax.random.fold_in(key, 6), dim), (blocks,), jnp.float32, smallest / len(shards), top_value / len(shards))
        return jnp.repeat(jnp.exp(steps), extent[dim] // blocks).reshape((-1,) + (1,) * (len(extent) - dim - 1))

    factor_of = one(*shards[0])
    for cut in shards[1:]:
        factor_of = factor_of * one(*cut)
    return factor_of


def gaussian(key, shape, scale, reach, pieces=(), kind=jnp.bfloat16):
    values = scale * jax.random.normal(key, shape, jnp.float32)
    if pieces:
        values = values * block_levels(key, shape, pieces, -0.22, 0.18)
    return jnp.clip(values, -reach, reach).astype(kind)


def setup_inputs(seed: int = 0) -> dict:
    streams_of = jax.random.split(jax.random.key(seed), 14)
    return {
        "loader_rows": draw_loader_rows(jax.random.fold_in(streams_of[13], 71), 0),
        "load_owner": draw_load_owner(jax.random.fold_in(streams_of[13], 71), 0),
        "load_slot": draw_load_slot(jax.random.fold_in(streams_of[13], 71), 0),
        "valid_frames": place_ends(jax.random.randint(streams_of[3], (STREAMS,), 1, FRAMES + 1), jax.random.fold_in(streams_of[3], 1), 1, FRAMES).astype(jnp.int32),
        "next_owner": draw_next_owner(jax.random.fold_in(streams_of[13], 71), 0),
        "pixel_cache": gaussian(streams_of[5], (STREAMS, 2, ROWS, 3 * COLS), 1.5, 6.0, ((0, 64), (2, 4))),
        "act_cache": gaussian(streams_of[6], (STREAMS, 2, ROWS, COLS, C1), 0.7, 4.0, ((0, 64), (2, 4))),
        "res_cache": gaussian(streams_of[7], (STREAMS, 2, ROWS, COLS, C1), 1.5, 8.0, ((0, 64), (2, 4))),
        "stem_weight": gaussian(streams_of[8], (3, 3, 3, 3, C1), 81 ** -0.5, 0.625),
        "norm_gain": jnp.clip(1.0 + 0.18 * jax.random.normal(streams_of[9], (C1,), jnp.float32), 0.1, 1.9),
        "norm_bias": gaussian(streams_of[10], (C1,), 0.5, 2.5, (), jnp.float32),
        "conv_weight": gaussian(streams_of[11], (3, 3, 3, C1, C1), (27 * C1) ** -0.5, 0.109375),
        "down_weight": gaussian(streams_of[12], (3, 3, 3, C1, C2), (27 * C1) ** -0.5, 0.109375),
    }


EPSILON = 1e-06

def conv_same(padded, weight):
    frame_count = padded.shape[0] - 2
    row_count = padded.shape[1] - 2
    col_count = padded.shape[2] - 2
    summed = jnp.zeros((frame_count, row_count, col_count, weight.shape[-1]), jnp.float32)
    for tap_t in range(3):
        for tap_h in range(3):
            stacked = jnp.concatenate([padded[tap_t:tap_t + frame_count, tap_h:tap_h + row_count, tap_w:tap_w + col_count, :] for tap_w in range(3)], axis=-1).astype(jnp.float32)
            kernel = weight[tap_t, tap_h].reshape(-1, weight.shape[-1]).astype(jnp.float32)
            summed = summed + jnp.einsum('trwc,co->trwo', stacked, kernel)
    return summed

def conv_down(padded, weight):
    out_t = (padded.shape[0] - 2) // 2
    out_h = (padded.shape[1] - 1) // 2
    out_w = (padded.shape[2] - 1) // 2
    summed = jnp.zeros((out_t, out_h, out_w, weight.shape[-1]), jnp.float32)
    for tap_t in range(3):
        for tap_h in range(3):
            stacked = jnp.concatenate([padded[tap_t:tap_t + 2 * out_t:2, tap_h:tap_h + 2 * out_h:2, tap_w:tap_w + 2 * out_w:2, :] for tap_w in range(3)], axis=-1).astype(jnp.float32)
            kernel = weight[tap_t, tap_h].reshape(-1, weight.shape[-1]).astype(jnp.float32)
            summed = summed + jnp.einsum('trwc,co->trwo', stacked, kernel)
    return summed

def normalize(hidden_in, mean_val, inv_std, gain_row, offset_row):
    dims_in = hidden_in.shape
    grouped = hidden_in.astype(jnp.float32).reshape(dims_in[:-1] + (mean_val.shape[1], dims_in[-1] // mean_val.shape[1]))
    centered = (grouped - mean_val[:, None, None, :, None]) * inv_std[:, None, None, :, None]
    scaled = centered.reshape(dims_in) * gain_row + offset_row
    return jax.nn.silu(scaled).astype(jnp.bfloat16)

def encode_stream(operands, stem_weight, norm_gain, norm_bias, conv_weight, down_weight):
    pixels, valid_count, pixel_prior, act_prior, res_prior = operands
    full_pix = jnp.concatenate([pixel_prior, pixels], 0)
    new_pix = lax.dynamic_slice_in_dim(full_pix, valid_count, 2, 0)
    planes = full_pix.reshape(FRAMES + 2, ROWS, 3, COLS).transpose(0, 1, 3, 2)
    planes = jnp.pad(planes, ((0, 0), (1, 1), (1, 1), (0, 0)))
    stem_out = conv_same(planes, stem_weight).astype(jnp.bfloat16)
    grouped = stem_out.astype(jnp.float32).reshape(FRAMES, ROWS, COLS, GROUPS, C1 // GROUPS)
    cell_count = ROWS * COLS * (C1 // GROUPS)
    mean_val = lax.optimization_barrier(jnp.sum(grouped, axis=(1, 2, 4))) / cell_count
    inv_std = lax.rsqrt(lax.optimization_barrier(jnp.sum(grouped * grouped, axis=(1, 2, 4))) / cell_count - mean_val * mean_val + EPSILON)
    act_now = normalize(stem_out, mean_val, inv_std, norm_gain, norm_bias)
    full_act = jnp.concatenate([act_prior, act_now], 0)
    new_act = lax.dynamic_slice_in_dim(full_act, valid_count, 2, 0)
    padded_act = jnp.pad(full_act, ((0, 0), (1, 1), (1, 1), (0, 0)))
    res_out = (stem_out.astype(jnp.float32) + conv_same(padded_act, conv_weight)).astype(jnp.bfloat16)
    full_res = jnp.concatenate([res_prior, res_out], 0)
    new_res = lax.dynamic_slice_in_dim(full_res, valid_count, 2, 0)
    padded_res = jnp.pad(full_res, ((0, 0), (1, 0), (1, 0), (0, 0)))
    latent = conv_down(padded_res, down_weight)
    live_frame = 2 * jnp.arange(FRAMES // 2, dtype=jnp.int32) < valid_count
    latent = jnp.where(live_frame[:, None, None, None], latent, jnp.zeros((), jnp.float32)).astype(jnp.bfloat16)
    return (latent, new_pix, new_act, new_res)

def reference(loader_rows, load_owner, load_slot, valid_frames, next_owner, pixel_cache, act_cache, res_cache, stem_weight, norm_gain, norm_bias, conv_weight, down_weight):
    row_fill = FRAMES * R_DEV
    strip_of = jnp.broadcast_to((jnp.arange(FRAMES * ROWS, dtype=jnp.int32) // row_fill)[None, :], load_owner.shape)
    placed = jnp.zeros((STREAMS, N_STRIP, row_fill, 3 * COLS), jnp.bfloat16)
    placed = placed.at[load_owner, strip_of, load_slot].set(loader_rows)
    pixels = placed.reshape(STREAMS, N_STRIP, FRAMES, R_DEV, 3 * COLS).transpose(0, 2, 1, 3, 4).reshape(STREAMS, FRAMES, ROWS, 3 * COLS)

    def encoder(operands):
        return encode_stream(operands, stem_weight, norm_gain, norm_bias, conv_weight, down_weight)
    latents, new_pix, new_act, new_res = lax.map(encoder, (pixels, valid_frames, pixel_cache, act_cache, res_cache))
    next_pixel_cache = jnp.zeros_like(new_pix).at[next_owner].set(new_pix)
    next_act_cache = jnp.zeros_like(new_act).at[next_owner].set(new_act)
    next_res_cache = jnp.zeros_like(new_res).at[next_owner].set(new_res)
    return (latents, next_pixel_cache, next_act_cache, next_res_cache)
```

```python
import functools

import jax
import jax.numpy as jnp
from jax import lax
from jax.experimental import pallas as pl
from jax.experimental.pallas import tpu as pltpu
from jax.sharding import PartitionSpec as P

F32 = jnp.float32
BF16 = jnp.bfloat16
I32 = jnp.int32
MESH = pl.DeviceIdType.MESH
EPS = 1e-06

T = 8
YS = 16
NY = 20
W = 16
C1 = 128
C2 = 256
N = 64

OFFSETS = sorted(
    [(dy, dz, dx, dc) for dy in range(4) for dz in range(2) for dx in range(4) for dc in range(2)][1:],
    key=lambda o: -(min(o[0], 4 - o[0]) + o[1] + min(o[2], 4 - o[2])),
)


def dot(a, b):
    return lax.dot_general(a, b, (((1,), (0,)), ((), ())), preferred_element_type=F32)


def iota(shape, dim):
    return lax.broadcasted_iota(I32, shape, dim)


def onehot(mask):
    return jnp.where(mask, 1.0, 0.0).astype(BF16)


def group_sum(x):
    lane = iota(x.shape, 1)
    size = x.shape[1]
    x = x + jnp.where(lane % 2 == 0, pltpu.roll(x, size - 1, 1), pltpu.roll(x, 1, 1))
    return x + jnp.where(lane % 4 < 2, pltpu.roll(x, size - 2, 1), pltpu.roll(x, 2, 1))


def shifted(x, by):
    col = iota(x.shape, 1)
    rolled = pltpu.roll(x, by % W, 1)
    return jnp.where(col == (0 if by == 1 else W - 1), 0.0, rolled)


def kernel(
    rows_ref, owner_ref, slot_ref, v_ref, nown_ref, pixc_ref, actc_ref, resc_ref, sw_ref, gain_ref,
    bias_ref, cw_hbm, dw_hbm,
    lat_ref, pixo_ref, acto_ref, reso_ref,
    rx, lsend, lrecv, vmat, ph, wpad, bmat, stem, stat_s, stat_r, act, dmat, rown, hact, hres,
    cw, dw, p1s, p1r, p2s, p2r, a1s, a1r, a2s, r1s, r1r, r2s, perm,
    wsem, lsem, hsem, xsem, tsem, psem, asem, rsem,
):
    me = lax.axis_index("stream")
    strip = lax.axis_index("strip")
    pc, px, pz, py = lax.rem(me, 2), lax.rem(me // 2, 4), lax.rem(me // 8, 2), me // 16
    ids_y = [lax.rem(py + d, 4) * 16 for d in range(4)]
    ids_z = [lax.rem(pz + d, 2) * 8 for d in range(2)]
    ids_x = [lax.rem(px + d, 4) * 2 for d in range(4)]
    ids_c = [lax.rem(pc + d, 2) for d in range(2)]
    peers = [ids_y[o[0]] + ids_z[o[1]] + ids_x[o[2]] + ids_c[o[3]] for o in OFFSETS]
    up = lax.rem(strip + 3, 4)
    down = lax.rem(strip + 1, 4)

    bar = pltpu.get_barrier_semaphore()
    for p in peers:
        pl.semaphore_signal(bar, inc=1, device_id={"stream": p}, device_id_type=MESH)
    for d in range(1, 4):
        pl.semaphore_signal(bar, inc=1, device_id={"strip": lax.rem(strip + d, 4)}, device_id_type=MESH)
    weights = [pltpu.make_async_copy(cw_hbm, cw, wsem.at[0]), pltpu.make_async_copy(dw_hbm, dw, wsem.at[1])]
    for copy in weights:
        copy.start()

    rx[...] = jnp.zeros((128, 128), F32)
    rx[:, 0:48] = rows_ref[...].astype(F32)
    owner = owner_ref[...]
    named = jnp.where(owner == iota((N, 128), 0), 1.0, 0.0)
    ahead = onehot(iota((128, 128), 0) < iota((128, 128), 1))
    count = dot(named.astype(BF16), ahead)
    pick0 = jnp.where(count < 0.5, named, 0.0)
    pick1 = named - pick0
    rows = rx[...]
    both = jnp.concatenate([rows, pltpu.roll(rows, 48, 1)], axis=0).astype(BF16)
    send = dot(jnp.concatenate([pick0, pick1], axis=1).astype(BF16), both)
    slot = slot_ref[...].astype(F32)
    slot0 = jnp.sum(pick0 * slot, axis=1, keepdims=True)
    slot1 = jnp.sum(pick1 * slot, axis=1, keepdims=True)
    lane = iota((N, 128), 1)
    send = jnp.where(lane == 96, slot0, send)
    send = jnp.where(lane == 97, slot1, send)
    send = jnp.where(lane == 98, nown_ref[0].astype(F32), send)
    lsend[...] = send.reshape(N, 1, 128)

    wpad[...] = jnp.zeros(wpad.shape, F32)
    wpad[:, 0:3, :] = sw_ref[...].astype(F32)
    wp = wpad[...].reshape(9, 24, 128).astype(BF16)
    wide = jnp.concatenate([wp[i] for i in range(9)], axis=1)
    bw, bc, bk = iota((16, 3, 16, 24), 0), iota((16, 3, 16, 24), 1), iota((16, 3, 16, 24), 2)
    bl = iota((16, 3, 16, 24), 3)
    band = onehot((bl % 8 == bc) & (bk == bw + bl // 8 - 1)).reshape(768, 24)
    banded = dot(band, wide).astype(BF16)
    bmat[432:512, :] = jnp.zeros((80, 2048), BF16)
    for w in range(W):
        for tap in range(9):
            bmat[tap * 48 : tap * 48 + 48, w * 128 : w * 128 + 128] = banded[
                w * 48 : w * 48 + 48, tap * 128 : tap * 128 + 128
            ]
    vmat[...] = jnp.zeros((256, 128), F32)
    vmat[128:160, 0:48] = pixc_ref[...].astype(F32)
    dmat[...] = jnp.zeros(dmat.shape, F32)
    act[:, 0] = jnp.zeros((NY, W, 384), BF16)

    def put_act(y, f, value):
        act[pl.ds(y, value.shape[0]), f] = jnp.concatenate(
            [shifted(value, 1), value, shifted(value, -1)], axis=2
        ).astype(BF16)

    def put_res(y, f, value):
        n = value.shape[0]
        return n

    for f in range(2):
        put_act(2, f + 1, actc_ref[f].astype(F32))

    pl.semaphore_wait(bar, N - 1 + 3)

    def exchange(src, dst, sems):
        for p in peers:
            pltpu.make_async_remote_copy(
                src_ref=src.at[p], dst_ref=dst.at[me], send_sem=sems.at[0], recv_sem=sems.at[1],
                device_id={"stream": p}, device_id_type=MESH,
            ).start()
        pltpu.make_async_copy(src.at[me], dst.at[me], sems.at[1]).start()

    def arrived(dst, sems):
        pltpu.make_async_copy(dst, dst, sems.at[1]).wait()

    def drained(src, sems):
        part = src.at[pl.ds(0, N - 1)]
        pltpu.make_async_copy(part, part, sems.at[0]).wait()

    exchange(lsend, lrecv, lsem)

    halo = []

    def to_strip(src, dst, other, i):
        copy = pltpu.make_async_remote_copy(
            src_ref=src, dst_ref=dst, send_sem=hsem.at[0, i], recv_sem=hsem.at[1, i],
            device_id={"strip": other}, device_id_type=MESH,
        )
        copy.start()
        return copy

    for f in range(2):
        halo.append(to_strip(actc_ref.at[f, pl.ds(14, 2)], hact.at[f, pl.ds(0, 2)], down, 3 * f))
        halo.append(to_strip(actc_ref.at[f, pl.ds(0, 1)], hact.at[f, pl.ds(2, 1)], up, 3 * f + 1))
        halo.append(to_strip(resc_ref.at[f, pl.ds(15, 1)], hres.at[f], down, 3 * f + 2))

    arrived(lrecv, lsem)
    got = lrecv[...].reshape(N, 128)
    col = iota((N, 128), 1)
    row = iota((N, 128), 0)
    diag = jnp.where(col == row, got[:, 96:97], 0.0) + jnp.where(col == row + N, got[:, 97:98], 0.0)
    slots = jnp.sum(diag, axis=0, keepdims=True).astype(I32)
    place = (slots % 16) * 16 + slots // 16 + 2
    k2 = iota((1, 128), 1)
    place_c = jnp.where(k2 < 32, (k2 % 16) * 16 + k2 // 16, -1)
    place = jnp.concatenate([place, place_c], axis=1)
    put = onehot(iota((256, 256), 0) == place)
    vmat[0:64, :] = jnp.where(col < 48, got, 0.0)
    vmat[64:128, :] = jnp.where(col < 48, pltpu.roll(got, 80, 1), 0.0)
    pix = dot(put, vmat[...].astype(BF16)).astype(BF16)
    ph[3:19] = pix.reshape(16, 16, 128)
    ph[21:22] = jnp.zeros((1, 16, 128), BF16)
    down_pix = pltpu.make_async_remote_copy(
        src_ref=ph.at[pl.ds(16, 3)], dst_ref=ph.at[pl.ds(0, 3)], send_sem=xsem.at[0, 0], recv_sem=xsem.at[1, 0],
        device_id={"strip": down}, device_id_type=MESH,
    )
    up_pix = pltpu.make_async_remote_copy(
        src_ref=ph.at[pl.ds(3, 2)], dst_ref=ph.at[pl.ds(19, 2)], send_sem=xsem.at[0, 1], recv_sem=xsem.at[1, 1],
        device_id={"strip": up}, device_id_type=MESH,
    )
    down_pix.start()
    up_pix.start()

    v = jnp.clip(v_ref[0], 1, T)
    tgt = got[:, 98:99]
    k = iota((N, 512), 1)
    spread = jnp.where(k // 8 == iota((N, 512), 0), tgt * 8.0 + (k % 8).astype(F32), 0.0)
    tgt8 = jnp.sum(spread, axis=0, keepdims=True).astype(I32)
    perm[...] = onehot(iota((512, 512), 0) == tgt8)
    tgt1 = jnp.sum(jnp.where(col == row, tgt, 0.0), axis=0, keepdims=True).astype(I32)
    perm1 = onehot((iota((N, 128), 0) == tgt1) & (iota((N, 128), 1) < N))
    pi, pq = iota((N, 256), 0), iota((N, 256), 1)
    sel = onehot((pq == (pi % 16) * 16 + v + pi // 16) & (pi < 32))
    p1s[...] = dot(sel, pix).reshape(N, 1, 128)
    exchange(p1s, p1r, psem.at[0])

    down_pix.wait()
    up_pix.wait()
    pf = ph[...].astype(F32)
    yy = iota((22, 16, 128), 0)
    live = ((yy >= 3) | (strip > 0)) & ((yy < 19) | (strip < 3))
    pf = jnp.where(live, pf, 0.0)
    ll = iota((NY * 8, 128), 1)
    parts = [jnp.zeros((NY * 8, 128), F32) for _ in range(4)]
    for a in range(3):
        xa = pf[:, a : a + 8, :]
        for b in range(3):
            x = xa[b : b + NY].reshape(NY * 8, 128)
            off = 48 * (3 * a + b)
            q, r = off // 128, off % 128
            if r:
                x = pltpu.roll(x, r, 1)
            if r + 48 > 128:
                parts[q] = parts[q] + jnp.where(ll >= r, x, 0.0)
                parts[q + 1] = parts[q + 1] + jnp.where(ll < r, x, 0.0)
            else:
                parts[q] = parts[q] + x
    lhs = jnp.concatenate(parts, axis=1).astype(BF16)
    s1 = jnp.zeros((8, 128), F32)
    s2 = jnp.zeros((8, 128), F32)
    for w in range(0, W, 2):
        pair = dot(lhs, bmat[:, w * 128 : w * 128 + 256]).astype(BF16).astype(F32)
        for h in range(2):
            block = pair[:, h * 128 : h * 128 + 128]
            stem[pl.ds(w + h, NY * 8, stride=W), :] = block
            own = block.reshape(NY, 8, 128)[2:18]
            s1 = s1 + jnp.sum(own, axis=0)
            s2 = s2 + jnp.sum(own * own, axis=0)
    stat_s[0:8] = s1
    stat_s[8:16] = s2
    stats = []
    for d in range(1, 4):
        copy = pltpu.make_async_remote_copy(
            src_ref=stat_s, dst_ref=stat_r.at[d - 1], send_sem=tsem.at[0, d - 1], recv_sem=tsem.at[1, d - 1],
            device_id={"strip": lax.rem(strip + d, 4)}, device_id_type=MESH,
        )
        copy.start()
        stats.append(copy)

    arrived(p1r, psem.at[0])
    p1 = jnp.concatenate([p1r[...].reshape(N, 128), jnp.zeros((N, 128), F32)], axis=0).astype(BF16)
    p2s[...] = dot(perm1, p1).reshape(N, 1, 128)
    exchange(p2s, p2r, psem.at[1])
    for copy in halo:
        copy.wait()
    for f in range(2):
        ha = hact[f].astype(F32)
        put_act(0, f + 1, jnp.where(strip > 0, ha[0:2], 0.0))
        put_act(18, f + 1, jnp.where(strip < 3, ha[2:3], 0.0))
    for copy in weights:
        copy.wait()

    for copy in stats:
        copy.wait()
    both = stat_s[...] + stat_r[0] + stat_r[1] + stat_r[2]
    both = group_sum(both) * (1.0 / (64 * 16 * 4))
    mean = both[0:8]
    inv = lax.rsqrt(both[8:16] - mean * mean + EPS)
    gain = inv * gain_ref[...]
    bias = bias_ref[...] - mean * gain
    gain = gain.reshape(8, 1, 128)
    bias = bias.reshape(8, 1, 128)

    def act_row(y, carry):
        s = stem[pl.ds(y * 128, 128), :].reshape(8, W, 128)
        u = s * gain + bias
        u = u / (1.0 + jnp.exp(-u))
        inside = ((y >= 2) | (strip > 0)) & ((y < 18) | (strip < 3))
        u = jnp.where(inside, u, 0.0)
        act[y, 3:11] = jnp.concatenate([shifted(u, 1), u, shifted(u, -1)], axis=2).astype(BF16)
        return carry

    lax.fori_loop(0, NY - 1, act_row, 0)

    picked = act[2:18, pl.ds(v + 1, 2), :, 128:256]
    for f in range(2):
        a1s[f * 32 : f * 32 + 32] = picked[:, f].astype(F32).reshape(32, 8, 128).astype(BF16)
    exchange(a1s, a1r, asem.at[0])

    def taps(ref_slice):
        return jnp.concatenate([ref_slice(a, b) for a in range(3) for b in range(3)], axis=1)

    def picked_taps(a, b):
        return act[1 + b : 17 + b, pl.ds(v - 1 + a, 2)].reshape(16 * 2 * W, 384)

    st = stem[...].reshape(NY, 8, W, 128)
    extra = dot(taps(picked_taps)[...], cw[...]).reshape(16, 2, W, 128)
    for f in range(2):
        t = jnp.maximum(v - 2 + f, 0)
        base = jnp.zeros((16, W, 128), F32)
        for i in range(8):
            base = jnp.where(t == i, st[2:18, i], base)
        new = (extra[:, f] + base).astype(BF16).astype(F32)
        if f == 0:
            new = jnp.where(v == 1, resc_ref[1].astype(F32), new)
        r1s[f * 32 : f * 32 + 32] = new.reshape(32, 8, 128).astype(BF16)
    exchange(r1s, r1r, rsem.at[0])

    def all_taps(a, b):
        return act[b + 0 : b + 17, 1 + a : 9 + a].reshape(17 * 8 * W, 384)

    res = dot(taps(all_taps), cw[...]).reshape(17, 8, W, 128)
    res = (res + st[1:18]).astype(BF16).astype(F32)
    keep = (iota((17, 8, W, 128), 0) > 0) | (strip > 0)
    res = jnp.where(keep, res, 0.0)
    rown[:, 2:10] = res
    for f in range(2):
        rown[1:17, f] = resc_ref[f].astype(F32)
        rown[0:1, f] = jnp.where(strip > 0, hres[f].astype(F32), 0.0)

    arrived(a1r, asem.at[0])
    a2s[...] = dot(perm[...], a1r[...].astype(F32).reshape(512, 128).astype(BF16)).reshape(N, 8, 128).astype(BF16)
    exchange(a2s, acto_ref, asem.at[1])
    arrived(r1r, rsem.at[0])
    r2s[...] = dot(perm[...], r1r[...].astype(F32).reshape(512, 128).astype(BF16)).reshape(N, 8, 128).astype(BF16)
    exchange(r2s, reso_ref, rsem.at[1])

    zero = jnp.zeros((1,), F32)
    del zero
    flat = rown.reshape(17 * 10 * W, 128)
    even = flat[pl.ds(0, 17 * 10 * 8, stride=2), :].reshape(170, 8, 128)
    odd = flat[pl.ds(1, 17 * 10 * 8, stride=2), :].reshape(170, 8, 128)
    before = jnp.where(iota((170, 8, 128), 1) == 0, 0.0, pltpu.roll(odd, 1, 1))
    full = jnp.concatenate([before, even, odd], axis=2).reshape(17, 10, 8, 384)
    for y in range(17):
        for f in range(10):
            dmat[y // 2, y % 2, f % 2, f // 2] = full[y, f]

    def down_taps(a, b):
        return dmat[b // 2 : b // 2 + 8, b % 2, a % 2, a // 2 : a // 2 + 4].reshape(256, 384).astype(BF16)

    lat = dot(taps(down_taps), dw[...]).reshape(8, 4, 8, 256)
    for t in range(4):
        lat_ref[t] = jnp.where(2 * t < v, lat[:, t], 0.0).astype(BF16)

    arrived(p2r, psem.at[1])
    pixo_ref[...] = p2r[...].reshape(N, 128)[0:32, 0:48].astype(BF16)
    drained(lsend, lsem)
    drained(p1s, psem.at[0])
    drained(p2s, psem.at[1])
    drained(a1s, asem.at[0])
    drained(r1s, rsem.at[0])
    drained(a2s, asem.at[1])
    drained(r2s, rsem.at[1])
    arrived(acto_ref, asem.at[1])
    arrived(reso_ref, rsem.at[1])


def body(
    loader_rows, load_owner, load_slot, valid_frames, next_owner, pixel_cache, act_cache, res_cache,
    stem_weight, norm_gain, norm_bias, conv_weight, down_weight,
):
    vm = pl.BlockSpec(memory_space=pltpu.VMEM)
    sm = pl.BlockSpec(memory_space=pltpu.SMEM)
    hbm = pl.BlockSpec(memory_space=pl.ANY)
    dma = pltpu.SemaphoreType.DMA
    lat, pix, act, res = pl.pallas_call(
        kernel,
        out_shape=(
            jax.ShapeDtypeStruct((4, 8, 8, C2), BF16),
            jax.ShapeDtypeStruct((32, 48), BF16),
            jax.ShapeDtypeStruct((N, 8, 128), BF16),
            jax.ShapeDtypeStruct((N, 8, 128), BF16),
        ),
        in_specs=[vm, vm, vm, sm, sm, vm, vm, vm, vm, vm, vm, hbm, hbm],
        out_specs=(vm, vm, vm, vm),
        scratch_shapes=[
            pltpu.VMEM((128, 128), F32),
            pltpu.VMEM((N, 1, 128), F32),
            pltpu.VMEM((N, 1, 128), F32),
            pltpu.VMEM((256, 128), F32),
            pltpu.VMEM((22, 16, 128), BF16),
            pltpu.VMEM((27, 8, 128), F32),
            pltpu.VMEM((512, 2048), BF16),
            pltpu.VMEM((NY * 8 * W, 128), F32),
            pltpu.VMEM((16, 128), F32),
            pltpu.VMEM((3, 16, 128), F32),
            pltpu.VMEM((NY, 11, W, 384), BF16),
            pltpu.VMEM((9, 2, 2, 5, 8, 384), F32),
            pltpu.VMEM((17, 10, W, 128), F32),
            pltpu.VMEM((2, 3, W, 128), BF16),
            pltpu.VMEM((2, 1, W, 128), BF16),
            pltpu.VMEM((3456, C1), BF16),
            pltpu.VMEM((3456, C2), BF16),
            pltpu.VMEM((N, 1, 128), F32),
            pltpu.VMEM((N, 1, 128), F32),
            pltpu.VMEM((N, 1, 128), F32),
            pltpu.VMEM((N, 1, 128), F32),
            pltpu.VMEM((N, 8, 128), BF16),
            pltpu.VMEM((N, 8, 128), BF16),
            pltpu.VMEM((N, 8, 128), BF16),
            pltpu.VMEM((N, 8, 128), BF16),
            pltpu.VMEM((N, 8, 128), BF16),
            pltpu.VMEM((N, 8, 128), BF16),
            pltpu.VMEM((512, 512), BF16),
            dma((2,)),
            dma((2,)),
            dma((2, 6)),
            dma((2, 2)),
            dma((2, 3)),
            dma((2, 2)),
            dma((2, 2)),
            dma((2, 2)),
        ],
        compiler_params=pltpu.CompilerParams(
            collective_id=0, has_side_effects=True, vmem_limit_bytes=60 * 1024 * 1024
        ),
        name="encoder",
    )(
        loader_rows[0], load_owner, load_slot, valid_frames, next_owner,
        pixel_cache.reshape(32, 48), act_cache[0], res_cache[0], stem_weight.reshape(27, 3, 128),
        norm_gain[None], norm_bias[None], conv_weight.reshape(3456, C1), down_weight.reshape(3456, C2),
    )
    return (
        lat[None],
        pix.reshape(1, 2, 16, 48),
        act.reshape(1, 2, 16, 16, 128),
        res.reshape(1, 2, 16, 16, 128),
    )


def solution(mesh):
    in_specs = (
        P("stream", "strip", None),
        P("stream", "strip"),
        P("stream", "strip"),
        P("stream"),
        P("stream"),
        P("stream", None, "strip", None),
        P("stream", None, "strip", None, None),
        P("stream", None, "strip", None, None),
        P(),
        P(),
        P(),
        P(),
        P(),
    )
    out_specs = (
        P("stream", None, "strip", None, None),
        P("stream", None, "strip", None),
        P("stream", None, "strip", None, None),
        P("stream", None, "strip", None, None),
    )
    return jax.shard_map(body, mesh=mesh, in_specs=in_specs, out_specs=out_specs, check_vma=False)
```

```python
import functools

import jax
import jax.numpy as jnp
from jax import lax
from jax.experimental import pallas as pl
from jax.experimental.pallas import tpu as pltpu
from jax.sharding import PartitionSpec as P

F32 = jnp.float32
BF16 = jnp.bfloat16
I32 = jnp.int32
MESH = pl.DeviceIdType.MESH
EPS = 1e-06

T = 8
YS = 16
NY = 20
W = 16
C1 = 128
C2 = 256
N = 64

OFFSETS = sorted(
    [(dy, dz, dx, dc) for dy in range(4) for dz in range(2) for dx in range(4) for dc in range(2)][1:],
    key=lambda o: -(min(o[0], 4 - o[0]) + o[1] + min(o[2], 4 - o[2])),
)


def dot(a, b):
    return lax.dot_general(a, b, (((1,), (0,)), ((), ())), preferred_element_type=F32)


def iota(shape, dim):
    return lax.broadcasted_iota(I32, shape, dim)


def onehot(mask):
    return jnp.where(mask, 1.0, 0.0).astype(BF16)


def group_sum(x):
    lane = iota(x.shape, 1)
    size = x.shape[1]
    x = x + jnp.where(lane % 2 == 0, pltpu.roll(x, size - 1, 1), pltpu.roll(x, 1, 1))
    return x + jnp.where(lane % 4 < 2, pltpu.roll(x, size - 2, 1), pltpu.roll(x, 2, 1))


def shifted(x, by):
    col = iota(x.shape, 1)
    rolled = pltpu.roll(x, by % W, 1)
    return jnp.where(col == (0 if by == 1 else W - 1), 0.0, rolled)


def kernel(
    v_ref, nown_ref, *refs,
):
    fetched, rest = refs[:11], refs[11:]
    work(v_ref, nown_ref, fetched, *rest)


def work(
    v_ref, nown_ref, fetched,
    lat_ref, pixo_ref, acto_ref, reso_ref,
    rows_ref, owner_ref, slot_ref, pixc_ref, sw_ref, gain_ref, bias_ref, actc_ref, resc_ref, cw, dw,
    rx, lsend, lrecv, vmat, ph, wpad, bmat, stem, stat_s, stat_r, act, dmat, rown, hact, hres,
    p1s, p1r, p2s, p2r, a1s, a1r, a2s, r1s, r1r, r2s, perm,
    wsem, lsem, hsem, xsem, tsem, psem, asem, rsem,
):
    me = lax.axis_index("stream")
    strip = lax.axis_index("strip")
    pc, px, pz, py = lax.rem(me, 2), lax.rem(me // 2, 4), lax.rem(me // 8, 2), me // 16
    ids_y = [lax.rem(py + d, 4) * 16 for d in range(4)]
    ids_z = [lax.rem(pz + d, 2) * 8 for d in range(2)]
    ids_x = [lax.rem(px + d, 4) * 2 for d in range(4)]
    ids_c = [lax.rem(pc + d, 2) for d in range(2)]
    peers = [ids_y[o[0]] + ids_z[o[1]] + ids_x[o[2]] + ids_c[o[3]] for o in OFFSETS]
    up = lax.rem(strip + 3, 4)
    down = lax.rem(strip + 1, 4)

    bar = pltpu.get_barrier_semaphore()
    for p in peers:
        pl.semaphore_signal(bar, inc=1, device_id={"stream": p}, device_id_type=MESH)
    for d in range(1, 4):
        pl.semaphore_signal(bar, inc=1, device_id={"strip": lax.rem(strip + d, 4)}, device_id_type=MESH)
    homes = (rows_ref, owner_ref, slot_ref, pixc_ref, sw_ref, gain_ref, bias_ref, actc_ref, resc_ref, cw, dw)
    loads = [pltpu.make_async_copy(fetched[i], homes[i], wsem.at[i]) for i in range(11)]
    for copy in loads:
        copy.start()
    weights = loads[9:]
    for copy in loads[:9]:
        copy.wait()

    rx[...] = jnp.zeros((128, 256), BF16)
    rx[0:48, 0:128] = rows_ref[...]
    rx[48:96, 128:256] = rows_ref[...]
    owner = owner_ref[...]
    named = jnp.where(owner == iota((N, 128), 0), 1.0, 0.0)
    ahead = onehot(iota((128, 128), 0) < iota((128, 128), 1))
    count = dot(named.astype(BF16), ahead)
    pick0 = jnp.where(count < 0.5, named, 0.0)
    pick1 = named - pick0
    picks = jnp.concatenate([pick0, pick1], axis=1).astype(BF16)
    send = lax.dot_general(picks, rx[...], (((1,), (1,)), ((), ())), preferred_element_type=F32)
    slot = slot_ref[...].astype(F32)
    slot0 = jnp.sum(pick0 * slot, axis=1, keepdims=True)
    slot1 = jnp.sum(pick1 * slot, axis=1, keepdims=True)
    lane = iota((N, 128), 1)
    send = jnp.where(lane == 96, slot0, send)
    send = jnp.where(lane == 97, slot1, send)
    send = jnp.where(lane == 98, nown_ref[0].astype(F32), send)
    lsend[...] = send.reshape(N, 1, 128)

    wpad[...] = jnp.zeros(wpad.shape, F32)
    wpad[:, 0:3, :] = sw_ref[...].astype(F32)
    wp = wpad[...].reshape(9, 24, 128).astype(BF16)
    wide = jnp.concatenate([wp[i] for i in range(9)], axis=1)
    bw, bc, bk = iota((16, 3, 16, 24), 0), iota((16, 3, 16, 24), 1), iota((16, 3, 16, 24), 2)
    bl = iota((16, 3, 16, 24), 3)
    band = onehot((bl % 8 == bc) & (bk == bw + bl // 8 - 1)).reshape(768, 24)
    banded = dot(band, wide).astype(BF16)
    bmat[432:512, :] = jnp.zeros((80, 2048), BF16)
    for w in range(W):
        for tap in range(9):
            bmat[tap * 48 : tap * 48 + 48, w * 128 : w * 128 + 128] = banded[
                w * 48 : w * 48 + 48, tap * 128 : tap * 128 + 128
            ]
    vmat[...] = jnp.zeros((256, 128), F32)
    vmat[128:160, 0:48] = pixc_ref[...].astype(F32)
    dmat[...] = jnp.zeros(dmat.shape, F32)
    act[:, 0] = jnp.zeros((NY, W, 384), BF16)

    def put_act(y, f, value):
        act[pl.ds(y, value.shape[0]), f] = jnp.concatenate(
            [shifted(value, 1), value, shifted(value, -1)], axis=2
        ).astype(BF16)

    def put_res(y, f, value):
        n = value.shape[0]
        return n

    for f in range(2):
        put_act(2, f + 1, actc_ref[f].astype(F32))

    pl.semaphore_wait(bar, N - 1 + 3)

    def exchange(src, dst, sems):
        for p in peers:
            pltpu.make_async_remote_copy(
                src_ref=src.at[p], dst_ref=dst.at[me], send_sem=sems.at[0], recv_sem=sems.at[1],
                device_id={"stream": p}, device_id_type=MESH,
            ).start()
        pltpu.make_async_copy(src.at[me], dst.at[me], sems.at[1]).start()

    def arrived(dst, sems):
        pltpu.make_async_copy(dst, dst, sems.at[1]).wait()

    def drained(src, sems):
        part = src.at[pl.ds(0, N - 1)]
        pltpu.make_async_copy(part, part, sems.at[0]).wait()

    exchange(lsend, lrecv, lsem)

    halo = []

    def to_strip(src, dst, other, i):
        copy = pltpu.make_async_remote_copy(
            src_ref=src, dst_ref=dst, send_sem=hsem.at[0, i], recv_sem=hsem.at[1, i],
            device_id={"strip": other}, device_id_type=MESH,
        )
        copy.start()
        return copy

    for f in range(2):
        halo.append(to_strip(actc_ref.at[f, pl.ds(14, 2)], hact.at[f, pl.ds(0, 2)], down, 3 * f))
        halo.append(to_strip(actc_ref.at[f, pl.ds(0, 1)], hact.at[f, pl.ds(2, 1)], up, 3 * f + 1))
        halo.append(to_strip(resc_ref.at[f, pl.ds(15, 1)], hres.at[f], down, 3 * f + 2))

    arrived(lrecv, lsem)
    got = lrecv[...].reshape(N, 128)
    col = iota((N, 128), 1)
    row = iota((N, 128), 0)
    diag = jnp.where(col == row, got[:, 96:97], 0.0) + jnp.where(col == row + N, got[:, 97:98], 0.0)
    slots = jnp.sum(diag, axis=0, keepdims=True).astype(I32)
    place = (slots % 16) * 16 + slots // 16 + 2
    k2 = iota((1, 128), 1)
    place_c = jnp.where(k2 < 32, (k2 % 16) * 16 + k2 // 16, -1)
    place = jnp.concatenate([place, place_c], axis=1)
    put = onehot(iota((256, 256), 0) == place)
    vmat[0:64, :] = jnp.where(col < 48, got, 0.0)
    vmat[64:128, :] = jnp.where(col < 48, pltpu.roll(got, 80, 1), 0.0)
    pix = dot(put, vmat[...].astype(BF16)).astype(BF16)
    ph[3:19] = pix.reshape(16, 16, 128)
    ph[21:22] = jnp.zeros((1, 16, 128), BF16)
    down_pix = pltpu.make_async_remote_copy(
        src_ref=ph.at[pl.ds(16, 3)], dst_ref=ph.at[pl.ds(0, 3)], send_sem=xsem.at[0, 0], recv_sem=xsem.at[1, 0],
        device_id={"strip": down}, device_id_type=MESH,
    )
    up_pix = pltpu.make_async_remote_copy(
        src_ref=ph.at[pl.ds(3, 2)], dst_ref=ph.at[pl.ds(19, 2)], send_sem=xsem.at[0, 1], recv_sem=xsem.at[1, 1],
        device_id={"strip": up}, device_id_type=MESH,
    )
    down_pix.start()
    up_pix.start()

    v = jnp.clip(v_ref[0], 1, T)
    tgt = got[:, 98:99]
    k = iota((N, 512), 1)
    spread = jnp.where(k // 8 == iota((N, 512), 0), tgt * 8.0 + (k % 8).astype(F32), 0.0)
    tgt8 = jnp.sum(spread, axis=0, keepdims=True).astype(I32)
    perm[...] = onehot(iota((512, 512), 0) == tgt8)
    tgt1 = jnp.sum(jnp.where(col == row, tgt, 0.0), axis=0, keepdims=True).astype(I32)
    perm1 = onehot((iota((N, 128), 0) == tgt1) & (iota((N, 128), 1) < N))
    pi, pq = iota((N, 256), 0), iota((N, 256), 1)
    sel = onehot((pq == (pi % 16) * 16 + v + pi // 16) & (pi < 32))
    p1s[...] = dot(sel, pix).reshape(N, 1, 128)
    exchange(p1s, p1r, psem.at[0])

    down_pix.wait()
    up_pix.wait()
    pf = ph[...].astype(F32)
    yy = iota((22, 16, 128), 0)
    live = ((yy >= 3) | (strip > 0)) & ((yy < 19) | (strip < 3))
    pf = jnp.where(live, pf, 0.0)
    ll = iota((NY * 8, 128), 1)
    parts = [jnp.zeros((NY * 8, 128), F32) for _ in range(4)]
    for a in range(3):
        xa = pf[:, a : a + 8, :]
        for b in range(3):
            x = xa[b : b + NY].reshape(NY * 8, 128)
            off = 48 * (3 * a + b)
            q, r = off // 128, off % 128
            if r:
                x = pltpu.roll(x, r, 1)
            if r + 48 > 128:
                parts[q] = parts[q] + jnp.where(ll >= r, x, 0.0)
                parts[q + 1] = parts[q + 1] + jnp.where(ll < r, x, 0.0)
            else:
                parts[q] = parts[q] + x
    lhs = jnp.concatenate(parts, axis=1).astype(BF16)
    stem_flat = stem.reshape(NY * 8 * W, 128)
    s1 = jnp.zeros((8, 128), F32)
    s2 = jnp.zeros((8, 128), F32)
    for w in range(0, W, 2):
        pair = dot(lhs, bmat[:, w * 128 : w * 128 + 256]).astype(BF16).astype(F32)
        for h in range(2):
            block = pair[:, h * 128 : h * 128 + 128]
            stem_flat[pl.ds(w + h, NY * 8, stride=W), :] = block
            own = block.reshape(NY, 8, 128)[2:18]
            s1 = s1 + jnp.sum(own, axis=0)
            s2 = s2 + jnp.sum(own * own, axis=0)
    stat_s[0:8] = s1
    stat_s[8:16] = s2
    stats = []
    for d in range(1, 4):
        copy = pltpu.make_async_remote_copy(
            src_ref=stat_s, dst_ref=stat_r.at[d - 1], send_sem=tsem.at[0, d - 1], recv_sem=tsem.at[1, d - 1],
            device_id={"strip": lax.rem(strip + d, 4)}, device_id_type=MESH,
        )
        copy.start()
        stats.append(copy)

    arrived(p1r, psem.at[0])
    p1 = jnp.concatenate([p1r[...].reshape(N, 128), jnp.zeros((N, 128), F32)], axis=0).astype(BF16)
    p2s[...] = dot(perm1, p1).reshape(N, 1, 128)
    exchange(p2s, p2r, psem.at[1])
    for copy in halo:
        copy.wait()
    for f in range(2):
        ha = hact[f].astype(F32)
        put_act(0, f + 1, jnp.where(strip > 0, ha[0:2], 0.0))
        put_act(18, f + 1, jnp.where(strip < 3, ha[2:3], 0.0))
    for copy in weights:
        copy.wait()

    for copy in stats:
        copy.wait()
    both = stat_s[...] + stat_r[0] + stat_r[1] + stat_r[2]
    both = group_sum(both) * (1.0 / (64 * 16 * 4))
    mean = both[0:8]
    inv = lax.rsqrt(both[8:16] - mean * mean + EPS)
    gain = inv * gain_ref[...]
    bias = bias_ref[...] - mean * gain
    gain = gain.reshape(8, 1, 128)
    bias = bias.reshape(8, 1, 128)

    def act_row(y, carry):
        s = stem[y]
        u = s * gain + bias
        u = u / (1.0 + jnp.exp(-u))
        inside = ((y >= 2) | (strip > 0)) & ((y < 18) | (strip < 3))
        u = jnp.where(inside, u, 0.0)
        act[y, 3:11] = jnp.concatenate([shifted(u, 1), u, shifted(u, -1)], axis=2).astype(BF16)
        return carry

    lax.fori_loop(0, NY, act_row, 0, unroll=4)

    picked = act[2:18, pl.ds(v + 1, 2), :, 128:256]
    for f in range(2):
        a1s[f * 32 : f * 32 + 32] = picked[:, f].astype(F32).reshape(32, 8, 128).astype(BF16)
    exchange(a1s, a1r, asem.at[0])

    def taps(ref_slice):
        return jnp.concatenate([ref_slice(a, b) for a in range(3) for b in range(3)], axis=1)

    def picked_taps(a, b):
        return act[1 + b : 17 + b, pl.ds(v - 1 + a, 2)].reshape(16 * 2 * W, 384)

    def conv(lhs):
        return dot(lhs[:, :1792], cw[:1792]) + dot(lhs[:, 1792:], cw[1792:])

    extra = conv(taps(picked_taps)).reshape(16, 2, W, 128)
    for f in range(2):
        base = stem[2:18, jnp.maximum(v - 2 + f, 0)]
        new = (extra[:, f] + base).astype(BF16).astype(F32)
        if f == 0:
            new = jnp.where(v == 1, resc_ref[1].astype(F32), new)
        r1s[f * 32 : f * 32 + 32] = new.reshape(32, 8, 128).astype(BF16)
    exchange(r1s, r1r, rsem.at[0])

    keep = (iota((17, 4, W, 128), 0) > 0) | (strip > 0)

    def half(h):
        def all_taps(a, b):
            return act[b : b + 17, 1 + a + 4 * h : 5 + a + 4 * h].reshape(17 * 4 * W, 384)

        res = conv(taps(all_taps)).reshape(17, 4, W, 128)
        res = (res + stem[1:18, 4 * h : 4 * h + 4]).astype(BF16).astype(F32)
        rown[:, 2 + 4 * h : 6 + 4 * h] = jnp.where(keep, res, 0.0)

    half(0)
    for f in range(2):
        rown[1:17, f] = resc_ref[f].astype(F32)
        rown[0:1, f] = jnp.where(strip > 0, hres[f].astype(F32), 0.0)

    arrived(a1r, asem.at[0])
    a2s[...] = dot(perm[...], a1r[...].astype(F32).reshape(512, 128).astype(BF16)).reshape(N, 8, 128).astype(BF16)
    exchange(a2s, acto_ref, asem.at[1])
    arrived(r1r, rsem.at[0])
    r2s[...] = dot(perm[...], r1r[...].astype(F32).reshape(512, 128).astype(BF16)).reshape(N, 8, 128).astype(BF16)
    exchange(r2s, reso_ref, rsem.at[1])

    half(1)

    zero = jnp.zeros((1,), F32)
    del zero
    flat = rown.reshape(17 * 10 * W, 128)
    even = flat[pl.ds(0, 17 * 10 * 8, stride=2), :].reshape(170, 8, 128)
    odd = flat[pl.ds(1, 17 * 10 * 8, stride=2), :].reshape(170, 8, 128)
    before = jnp.where(iota((170, 8, 128), 1) == 0, 0.0, pltpu.roll(odd, 1, 1))
    full = jnp.concatenate([before, even, odd], axis=2).reshape(17, 10, 8, 384)
    for y in range(17):
        for f in range(10):
            dmat[y // 2, y % 2, f % 2, f // 2] = full[y, f]

    def down_taps(a, b):
        return dmat[b // 2 : b // 2 + 8, b % 2, a % 2, a // 2 : a // 2 + 4].reshape(256, 384).astype(BF16)

    lat = dot(taps(down_taps), dw[...]).reshape(8, 4, 8, 256)
    for t in range(4):
        lat_ref[t] = jnp.where(2 * t < v, lat[:, t], 0.0).astype(BF16)

    arrived(p2r, psem.at[1])
    pixo_ref[...] = p2r[...].reshape(N, 128)[0:32, 0:48].astype(BF16)
    drained(lsend, lsem)
    drained(p1s, psem.at[0])
    drained(p2s, psem.at[1])
    drained(a1s, asem.at[0])
    drained(r1s, rsem.at[0])
    drained(a2s, asem.at[1])
    drained(r2s, rsem.at[1])
    arrived(acto_ref, asem.at[1])
    arrived(reso_ref, rsem.at[1])


def settle(*refs):
    count = len(refs) // 2
    sems = refs[-1]
    copies = [pltpu.make_async_copy(refs[i], refs[count + i], sems.at[i]) for i in range(count)]
    for copy in copies:
        copy.start()
    for copy in copies:
        copy.wait()


def body(
    loader_rows, load_owner, load_slot, valid_frames, next_owner, pixel_cache, act_cache, res_cache,
    stem_weight, norm_gain, norm_bias, conv_weight, down_weight,
):
    vm = pl.BlockSpec(memory_space=pltpu.VMEM)
    sm = pl.BlockSpec(memory_space=pltpu.SMEM)
    hbm = pl.BlockSpec(memory_space=pl.ANY)
    dma = pltpu.SemaphoreType.DMA
    shapes = ((4, 8, 8, C2), (32, 48), (N, 8, 128), (N, 8, 128))
    parts = pl.pallas_call(
        kernel,
        out_shape=tuple(pltpu.VMEM(s, BF16) for s in shapes),
        in_specs=[sm, sm] + [hbm] * 11,
        out_specs=(vm, vm, vm, vm),
        scratch_shapes=[
            pltpu.VMEM((48, 128), BF16),
            pltpu.VMEM((1, 128), I32),
            pltpu.VMEM((1, 128), I32),
            pltpu.VMEM((32, 48), BF16),
            pltpu.VMEM((27, 3, 128), BF16),
            pltpu.VMEM((1, 128), F32),
            pltpu.VMEM((1, 128), F32),
            pltpu.VMEM((2, 16, W, 128), BF16),
            pltpu.VMEM((2, 16, W, 128), BF16),
            pltpu.VMEM((3456, C1), BF16),
            pltpu.VMEM((3456, C2), BF16),
            pltpu.VMEM((128, 256), BF16),
            pltpu.VMEM((N, 1, 128), F32),
            pltpu.VMEM((N, 1, 128), F32),
            pltpu.VMEM((256, 128), F32),
            pltpu.VMEM((22, 16, 128), BF16),
            pltpu.VMEM((27, 8, 128), F32),
            pltpu.VMEM((512, 2048), BF16),
            pltpu.VMEM((NY, 8, W, 128), F32),
            pltpu.VMEM((16, 128), F32),
            pltpu.VMEM((3, 16, 128), F32),
            pltpu.VMEM((NY, 11, W, 384), BF16),
            pltpu.VMEM((9, 2, 2, 5, 8, 384), F32),
            pltpu.VMEM((17, 10, W, 128), F32),
            pltpu.VMEM((2, 3, W, 128), BF16),
            pltpu.VMEM((2, 1, W, 128), BF16),
            pltpu.VMEM((N, 1, 128), F32),
            pltpu.VMEM((N, 1, 128), F32),
            pltpu.VMEM((N, 1, 128), F32),
            pltpu.VMEM((N, 1, 128), F32),
            pltpu.VMEM((N, 8, 128), BF16),
            pltpu.VMEM((N, 8, 128), BF16),
            pltpu.VMEM((N, 8, 128), BF16),
            pltpu.VMEM((N, 8, 128), BF16),
            pltpu.VMEM((N, 8, 128), BF16),
            pltpu.VMEM((N, 8, 128), BF16),
            pltpu.VMEM((512, 512), BF16),
            dma((11,)),
            dma((2,)),
            dma((2, 6)),
            dma((2, 2)),
            dma((2, 3)),
            dma((2, 2)),
            dma((2, 2)),
            dma((2, 2)),
        ],
        compiler_params=pltpu.CompilerParams(
            collective_id=0, has_side_effects=True, vmem_limit_bytes=60 * 1024 * 1024
        ),
        name="encoder",
    )(
        valid_frames, next_owner, loader_rows[0].T, load_owner, load_slot,
        pixel_cache.reshape(32, 48), stem_weight.reshape(27, 3, 128), norm_gain[None], norm_bias[None],
        act_cache[0], res_cache[0], conv_weight.reshape(3456, C1), down_weight.reshape(3456, C2),
    )
    lat, pix, act, res = pl.pallas_call(
        settle,
        out_shape=tuple(jax.ShapeDtypeStruct(s, BF16) for s in shapes),
        in_specs=[hbm] * 4,
        out_specs=(hbm,) * 4,
        scratch_shapes=[dma((4,))],
        name="settle",
    )(*[pltpu.with_memory_space_constraint(p, pltpu.VMEM) for p in parts])
    return (
        lat[None],
        pix.reshape(1, 2, 16, 48),
        act.reshape(1, 2, 16, 16, 128),
        res.reshape(1, 2, 16, 16, 128),
    )


def solution(mesh):
    in_specs = (
        P("stream", "strip", None),
        P("stream", "strip"),
        P("stream", "strip"),
        P("stream"),
        P("stream"),
        P("stream", None, "strip", None),
        P("stream", None, "strip", None, None),
        P("stream", None, "strip", None, None),
        P(),
        P(),
        P(),
        P(),
        P(),
    )
    out_specs = (
        P("stream", None, "strip", None, None),
        P("stream", None, "strip", None),
        P("stream", None, "strip", None, None),
        P("stream", None, "strip", None, None),
    )
    return jax.shard_map(body, mesh=mesh, in_specs=in_specs, out_specs=out_specs, check_vma=False)
```

```python
import functools

import jax
import jax.numpy as jnp
from jax import lax
from jax.experimental import pallas as pl
from jax.experimental.pallas import tpu as pltpu
from jax.sharding import PartitionSpec as P

F32 = jnp.float32
BF16 = jnp.bfloat16
I32 = jnp.int32
MESH = pl.DeviceIdType.MESH
EPS = 1e-06

T = 8
YS = 16
NY = 20
W = 16
C1 = 128
C2 = 256
N = 64

OFFSETS = sorted(
    [(dy, dz, dx, dc) for dy in range(4) for dz in range(2) for dx in range(4) for dc in range(2)][1:],
    key=lambda o: -(min(o[0], 4 - o[0]) + o[1] + min(o[2], 4 - o[2])),
)


def dot(a, b):
    return lax.dot_general(a, b, (((1,), (0,)), ((), ())), preferred_element_type=F32)


def iota(shape, dim):
    return lax.broadcasted_iota(I32, shape, dim)


def onehot(mask):
    return jnp.where(mask, 1.0, 0.0).astype(BF16)


def group_sum(x):
    lane = iota(x.shape, 1)
    size = x.shape[1]
    x = x + jnp.where(lane % 2 == 0, pltpu.roll(x, size - 1, 1), pltpu.roll(x, 1, 1))
    return x + jnp.where(lane % 4 < 2, pltpu.roll(x, size - 2, 1), pltpu.roll(x, 2, 1))


def shifted(x, by):
    col = iota(x.shape, 1)
    rolled = pltpu.roll(x, by % W, 1)
    return jnp.where(col == (0 if by == 1 else W - 1), 0.0, rolled)


def kernel(
    v_ref, nown_ref, *refs,
):
    fetched, rest = refs[:13], refs[13:]
    work(v_ref, nown_ref, fetched, *rest)


def work(
    v_ref, nown_ref, fetched,
    lat_ref, pixo_ref, acto_ref, reso_ref,
    rows_ref, owner_ref, slot_ref, pixc_ref, sw_ref, gain_ref, bias_ref, actc_ref, resc_ref, cw01, cw2, dw,
    rx, lsend, lrecv, fsend, frecv, vmat, ph, fph, wpad, bmat, stem, fstem, stat_s, stat_r, fstat_s, fstat_r,
    act, fact, fcache, dmat, rown, hact, hres, fhact,
    a1s, a1r, a2s, a2r, r1s, r1r, r2s, r2r, perm,
    wsem, lsem, fsem, hsem, gsem, xsem, ysem, tsem, usem, asem, rsem,
):
    me = lax.axis_index("stream")
    strip = lax.axis_index("strip")
    pc, px, pz, py = lax.rem(me, 2), lax.rem(me // 2, 4), lax.rem(me // 8, 2), me // 16
    ids_y = [lax.rem(py + d, 4) * 16 for d in range(4)]
    ids_z = [lax.rem(pz + d, 2) * 8 for d in range(2)]
    ids_x = [lax.rem(px + d, 4) * 2 for d in range(4)]
    ids_c = [lax.rem(pc + d, 2) for d in range(2)]
    peers = [ids_y[o[0]] + ids_z[o[1]] + ids_x[o[2]] + ids_c[o[3]] for o in OFFSETS]
    up = lax.rem(strip + 3, 4)
    down = lax.rem(strip + 1, 4)

    bar = pltpu.get_barrier_semaphore()
    for p in peers:
        pl.semaphore_signal(bar, inc=1, device_id={"stream": p}, device_id_type=MESH)
    for d in range(1, 4):
        pl.semaphore_signal(bar, inc=1, device_id={"strip": lax.rem(strip + d, 4)}, device_id_type=MESH)
    homes = (
        rows_ref, owner_ref, slot_ref, pixc_ref, sw_ref, gain_ref, bias_ref, actc_ref, resc_ref, a1s, r1s
    )
    loads = [pltpu.make_async_copy(fetched[i], homes[i], wsem.at[i]) for i in range(11)]
    weights = [pltpu.make_async_copy(fetched[12], dw, wsem.at[11])]
    for a in range(3):
        rows = pl.ds(a * 384, 384)
        for b in range(3):
            home = cw2.at[rows] if b == 2 else cw01.at[rows, pl.ds(b * 128, 128)]
            weights.append(pltpu.make_async_copy(fetched[11].at[3 * a + b], home, wsem.at[12 + 3 * a + b]))
    for copy in loads + weights:
        copy.start()
    for copy in loads:
        copy.wait()
    v = jnp.clip(v_ref[0], 1, T)

    rx[...] = jnp.zeros((128, 256), BF16)
    rx[0:48, 0:128] = rows_ref[...]
    rx[48:96, 128:256] = rows_ref[...]
    owner = owner_ref[...]
    named = jnp.where(owner == iota((N, 128), 0), 1.0, 0.0)
    ahead = onehot(iota((128, 128), 0) < iota((128, 128), 1))
    count = dot(named.astype(BF16), ahead)
    pick0 = jnp.where(count < 0.5, named, 0.0)
    pick1 = named - pick0
    picks = jnp.concatenate([pick0, pick1], axis=1).astype(BF16)
    send = lax.dot_general(picks, rx[...], (((1,), (1,)), ((), ())), preferred_element_type=F32)
    slot = slot_ref[...].astype(F32)
    slot0 = jnp.sum(pick0 * slot, axis=1, keepdims=True)
    slot1 = jnp.sum(pick1 * slot, axis=1, keepdims=True)
    lane = iota((N, 128), 1)
    send = jnp.where(lane == 96, slot0, send)
    send = jnp.where(lane == 97, slot1, send)
    send = jnp.where(lane == 98, nown_ref[0].astype(F32), send)
    send = jnp.where(lane == 99, v.astype(F32), send)
    vmat[...] = jnp.zeros((256, 128), F32)
    vmat[128:160, 0:48] = pixc_ref[...].astype(F32)
    lsend[:, 0:1, :] = send.reshape(N, 1, 128)
    lsend[:, 1:2, :] = vmat[128:192].reshape(N, 1, 128)

    wpad[...] = jnp.zeros(wpad.shape, F32)
    wpad[:, 0:3, :] = sw_ref[...].astype(F32)
    wp = wpad[...].reshape(9, 24, 128).astype(BF16)
    wide = jnp.concatenate([wp[i] for i in range(9)], axis=1)
    bw, bc, bk = iota((16, 3, 16, 24), 0), iota((16, 3, 16, 24), 1), iota((16, 3, 16, 24), 2)
    bl = iota((16, 3, 16, 24), 3)
    band = onehot((bl % 8 == bc) & (bk == bw + bl // 8 - 1)).reshape(768, 24)
    banded = dot(band, wide).astype(BF16)
    bmat[432:512, :] = jnp.zeros((80, 2048), BF16)
    for w in range(W):
        for tap in range(9):
            bmat[tap * 48 : tap * 48 + 48, w * 128 : w * 128 + 128] = banded[
                w * 48 : w * 48 + 48, tap * 128 : tap * 128 + 128
            ]
    ph[21:22] = jnp.zeros((1, 16, 128), BF16)
    fph[21:22] = jnp.zeros((1, 16, 128), BF16)
    fcache[19:20] = jnp.zeros((1, 2, W, 128), F32)

    def three(value):
        return jnp.concatenate([shifted(value, 1), value, shifted(value, -1)], axis=2).astype(BF16)

    for f in range(2):
        act[2:18, f] = three(actc_ref[f].astype(F32))

    pl.semaphore_wait(bar, N - 1 + 3)

    def exchange(src, dst, sems):
        for p in peers:
            pltpu.make_async_remote_copy(
                src_ref=src.at[p], dst_ref=dst.at[me], send_sem=sems.at[0], recv_sem=sems.at[1],
                device_id={"stream": p}, device_id_type=MESH,
            ).start()
        pltpu.make_async_copy(src.at[me], dst.at[me], sems.at[1]).start()

    def arrived(dst, sems):
        pltpu.make_async_copy(dst, dst, sems.at[1]).wait()

    def drained(src, sems):
        part = src.at[pl.ds(0, N - 1)]
        pltpu.make_async_copy(part, part, sems.at[0]).wait()

    def to_strip(src, dst, other, sems, i):
        copy = pltpu.make_async_remote_copy(
            src_ref=src, dst_ref=dst, send_sem=sems.at[0, i], recv_sem=sems.at[1, i],
            device_id={"strip": other}, device_id_type=MESH,
        )
        copy.start()
        return copy

    exchange(lsend, lrecv, lsem)
    exchange(a1s, a1r, asem.at[0])
    exchange(r1s, r1r, rsem.at[0])
    halo = []
    for f in range(2):
        halo.append(to_strip(actc_ref.at[f, pl.ds(14, 2)], hact.at[f, pl.ds(0, 2)], down, hsem, 3 * f))
        halo.append(to_strip(actc_ref.at[f, pl.ds(0, 1)], hact.at[f, pl.ds(2, 1)], up, hsem, 3 * f + 1))
        halo.append(to_strip(resc_ref.at[f, pl.ds(15, 1)], hres.at[f], down, hsem, 3 * f + 2))

    col = iota((N, 128), 1)
    row = iota((N, 128), 0)

    def assemble(got, place, place_c):
        vmat[0:64, :] = jnp.where(col < 48, got, 0.0)
        vmat[64:128, :] = jnp.where(col < 48, pltpu.roll(got, 80, 1), 0.0)
        put = onehot(iota((256, 256), 0) == jnp.concatenate([place, place_c], axis=1))
        return dot(put, vmat[...].astype(BF16)).astype(BF16)

    def slots_of(got):
        diag = jnp.where(col == row, got[:, 96:97], 0.0) + jnp.where(col == row + N, got[:, 97:98], 0.0)
        return jnp.sum(diag, axis=0, keepdims=True).astype(I32)

    def rims(pixels, sems):
        return [
            to_strip(pixels.at[pl.ds(16, 3)], pixels.at[pl.ds(0, 3)], down, sems, 0),
            to_strip(pixels.at[pl.ds(3, 2)], pixels.at[pl.ds(19, 2)], up, sems, 1),
        ]

    def stem_of(pixels, out, sums):
        pf = pixels[...].astype(F32)
        yy = iota((22, 16, 128), 0)
        live = ((yy >= 3) | (strip > 0)) & ((yy < 19) | (strip < 3))
        pf = jnp.where(live, pf, 0.0)
        ll = iota((NY * 8, 128), 1)
        parts = [jnp.zeros((NY * 8, 128), F32) for _ in range(4)]
        for a in range(3):
            xa = pf[:, a : a + 8, :]
            for b in range(3):
                x = xa[b : b + NY].reshape(NY * 8, 128)
                off = 48 * (3 * a + b)
                q, r = off // 128, off % 128
                if r:
                    x = pltpu.roll(x, r, 1)
                if r + 48 > 128:
                    parts[q] = parts[q] + jnp.where(ll >= r, x, 0.0)
                    parts[q + 1] = parts[q + 1] + jnp.where(ll < r, x, 0.0)
                else:
                    parts[q] = parts[q] + x
        lhs = jnp.concatenate(parts, axis=1).astype(BF16)
        flat = out.reshape(NY * 8 * W, 128)
        s1 = jnp.zeros((8, 128), F32)
        s2 = jnp.zeros((8, 128), F32)
        for w in range(0, W, 2):
            pair = dot(lhs, bmat[:, w * 128 : w * 128 + 256]).astype(BF16).astype(F32)
            for h in range(2):
                block = pair[:, h * 128 : h * 128 + 128]
                flat[pl.ds(w + h, NY * 8, stride=W), :] = block
                own = block.reshape(NY, 8, 128)[2:18]
                s1 = s1 + jnp.sum(own, axis=0)
                s2 = s2 + jnp.sum(own * own, axis=0)
        sums[0:8] = s1
        sums[8:16] = s2

    def share(sums, others, sems):
        return [to_strip(sums, others.at[d - 1], lax.rem(strip + d, 4), sems, d - 1) for d in range(1, 4)]

    def scale_of(sums, others):
        both = sums[...] + others[0] + others[1] + others[2]
        both = group_sum(both) * (1.0 / (64 * 16 * 4))
        mean = both[0:8]
        inv = lax.rsqrt(both[8:16] - mean * mean + EPS)
        gain = inv * gain_ref[...]
        bias = bias_ref[...] - mean * gain
        return gain.reshape(8, 1, 128), bias.reshape(8, 1, 128)

    def silu_row(y, x, gain, bias):
        u = x * gain + bias
        u = u / (1.0 + jnp.exp(-u))
        return jnp.where(((y >= 2) | (strip > 0)) & ((y < 18) | (strip < 3)), u, 0.0)

    arrived(lrecv, lsem)
    got = lrecv[:, 0:1, :].reshape(N, 128)
    tgt = got[:, 98:99]
    tgt1 = jnp.sum(jnp.where(col == row, tgt, 0.0), axis=0, keepdims=True).astype(I32)
    perm1 = onehot((row == tgt1) & (col < N))
    blank = jnp.zeros((N, 128), F32)
    mine = jnp.concatenate([lsend[:, 0:1, :].reshape(N, 128), blank], axis=0).astype(BF16)
    theirs = jnp.concatenate([lrecv[:, 1:2, :].reshape(N, 128), blank], axis=0).astype(BF16)
    fsend[:, 0:1, :] = dot(perm1, mine).reshape(N, 1, 128)
    fsend[:, 1:2, :] = dot(perm1, theirs).reshape(N, 1, 128)
    exchange(fsend, frecv, fsem)
    fv = jnp.sum(jnp.where(tgt == me.astype(F32), got[:, 99:100] + jnp.zeros((N, 128), F32), 0.0), axis=0, keepdims=True)
    fv = fv.astype(I32)

    slots = slots_of(got)
    k2 = iota((1, 128), 1)
    pix = assemble(got, (slots % 16) * 16 + slots // 16 + 2, jnp.where(k2 < 32, (k2 % 16) * 16 + k2 // 16, -1))
    ph[3:19] = pix.reshape(16, 16, 128)
    pix_rims = rims(ph, xsem)

    k = iota((N, 512), 1)
    spread = jnp.where(k // 8 == iota((N, 512), 0), tgt * 8.0 + (k % 8).astype(F32), 0.0)
    tgt8 = jnp.sum(spread, axis=0, keepdims=True).astype(I32)
    perm[...] = onehot(iota((512, 512), 0) == tgt8)

    def onward(src, out):
        flat = src[...].astype(F32).reshape(512, 128).astype(BF16)
        out[...] = dot(perm[...], flat).reshape(N, 8, 128).astype(BF16)

    for copy in pix_rims:
        copy.wait()
    stem_of(ph, stem, stat_s)
    stats = share(stat_s, stat_r, tsem)
    arrived(a1r, asem.at[0])
    onward(a1r, a2s)
    exchange(a2s, a2r, asem.at[1])

    arrived(frecv, fsem)
    fgot = frecv[:, 0:1, :].reshape(N, 128)
    vmat[128:160] = frecv[:, 1:2, :].reshape(N, 128)[0:32]
    slots = slots_of(fgot)
    frame = slots // 16 + 6 - fv
    frame_c = k2 // 16 + 4 - fv
    place = jnp.where((frame >= 0) & (frame < 6), (slots % 16) * 16 + frame, -1)
    place_c = jnp.where((frame_c >= 0) & (k2 < 32), (k2 % 16) * 16 + frame_c, -1)
    fpix = assemble(fgot, place, place_c)
    fph[3:19] = fpix.reshape(16, 16, 128)
    fpix_rims = rims(fph, ysem)
    pi, pq = iota((N, 256), 0), iota((N, 256), 1)
    sel = onehot(pq == (pi % 16) * 16 + 4 + pi // 16)
    pixo_ref[...] = dot(sel, fpix)[0:32, 0:48].astype(BF16)

    for copy in weights:
        copy.wait()
    for copy in halo:
        copy.wait()
    for f in range(2):
        ha = hact[f].astype(F32)
        act[0:2, f] = three(jnp.where(strip > 0, ha[0:2], 0.0))
        act[18:19, f] = three(jnp.where(strip < 3, ha[2:3], 0.0))
        rown[1:17, f] = resc_ref[f].astype(F32)
        rown[0:1, f] = jnp.where(strip > 0, hres[f].astype(F32), 0.0)

    for copy in stats:
        copy.wait()
    gain, bias = scale_of(stat_s, stat_r)

    def act_row(y, carry):
        act[y, 2:10] = three(silu_row(y, stem[y], gain, bias))
        return carry

    lax.fori_loop(0, NY, act_row, 0, unroll=4)

    for copy in fpix_rims:
        copy.wait()
    stem_of(fph, fstem, fstat_s)
    fstats = share(fstat_s, fstat_r, usem)
    arrived(r1r, rsem.at[0])
    onward(r1r, r2s)
    exchange(r2s, r2r, rsem.at[1])

    arrived(a2r, asem.at[1])
    fhalo = []
    for f in range(2):
        fhalo.append(to_strip(a2r.at[pl.ds(f * 32 + 28, 4)], fhact.at[f, pl.ds(0, 4)], down, gsem, 2 * f))
        fhalo.append(to_strip(a2r.at[pl.ds(f * 32, 2)], fhact.at[f, pl.ds(4, 2)], up, gsem, 2 * f + 1))
        fcache[2:18, f] = a2r[f * 32 : f * 32 + 32].astype(F32).reshape(16, W, 128)

    def conv(x, first, count, frames):
        def lhs(y, n):
            return jnp.concatenate([x(y, n, a).reshape(n * frames * W, 384) for a in range(3)], axis=1)

        pair = dot(lhs(first, count + 1), cw01[...]).reshape(count + 1, frames, W, 256)
        last = dot(lhs(first + 2, count), cw2[...]).reshape(count, frames, W, 128)
        return pair[:count, :, :, :128] + pair[1:, :, :, 128:] + last

    def taps(ref_slice):
        return jnp.concatenate([ref_slice(a, b) for a in range(3) for b in range(3)], axis=1)

    keep = (iota((17, 4, W, 128), 0) > 0) | (strip > 0)

    def half(h):
        def rows(y, n, a):
            return act[y : y + n, a + 4 * h : 4 + a + 4 * h]

        res = conv(rows, 0, 17, 4)
        res = (res + stem[1:18, 4 * h : 4 * h + 4]).astype(BF16).astype(F32)
        rown[:, 2 + 4 * h : 6 + 4 * h] = jnp.where(keep, res, 0.0)

    half(0)
    half(1)

    for copy in fhalo:
        copy.wait()
    for f in range(2):
        ha = fhact[f].astype(F32).reshape(3, W, 128)
        fcache[0:2, f] = jnp.where(strip > 0, ha[0:2], 0.0)
        fcache[18:19, f] = jnp.where(strip < 3, ha[2:3], 0.0)
    for copy in fstats:
        copy.wait()
    fgain, fbias = scale_of(fstat_s, fstat_r)

    def fact_row(y, carry):
        u = silu_row(y, fstem[y, 0:4], fgain[0:4], fbias[0:4])
        c = fcache[y]
        u0 = jnp.where(fv == 2, c[0], jnp.where(fv == 3, c[1], u[0]))
        u1 = jnp.where(fv == 1, c[0], jnp.where(fv == 2, c[1], u[1]))
        u2 = jnp.where(fv == 1, c[1], u[2])
        fact[y] = three(jnp.stack([u0, u1, u2, u[3]]))
        return carry

    lax.fori_loop(0, NY, fact_row, 0, unroll=4)

    for f in range(2):
        acto_ref[f * 32 : f * 32 + 32] = (
            fact[2:18, 2 + f, :, 128:256].astype(F32).reshape(32, 8, 128).astype(BF16)
        )

    def next_rows(y, n, a):
        return fact[y : y + n, a : a + 2]

    arrived(r2r, rsem.at[1])
    extra = conv(next_rows, 1, 16, 2)
    for f in range(2):
        new = (extra[:, f] + fstem[2:18, 2 + f]).astype(BF16).astype(F32)
        if f == 0:
            new = jnp.where(fv == 1, r2r[32:64].astype(F32).reshape(16, W, 128), new)
        reso_ref[f * 32 : f * 32 + 32] = new.reshape(32, 8, 128).astype(BF16)

    flat = rown.reshape(17 * 10 * W, 128)
    even = flat[pl.ds(0, 17 * 10 * 8, stride=2), :].reshape(170, 8, 128)
    odd = flat[pl.ds(1, 17 * 10 * 8, stride=2), :].reshape(170, 8, 128)
    before = jnp.where(iota((170, 8, 128), 1) == 0, 0.0, pltpu.roll(odd, 1, 1))
    full = jnp.concatenate([before, even, odd], axis=2).reshape(17, 10, 8, 384)
    for y in range(17):
        for f in range(10):
            dmat[y // 2, y % 2, f % 2, f // 2] = full[y, f]

    def down_taps(a, b):
        return dmat[b // 2 : b // 2 + 8, b % 2, a % 2, a // 2 : a // 2 + 4].reshape(256, 384).astype(BF16)

    lat = dot(taps(down_taps), dw[...]).reshape(8, 4, 8, 256)
    for t in range(4):
        lat_ref[t] = jnp.where(2 * t < v, lat[:, t], 0.0).astype(BF16)

    drained(lsend, lsem)
    drained(fsend, fsem)
    drained(a1s, asem.at[0])
    drained(r1s, rsem.at[0])
    drained(a2s, asem.at[1])
    drained(r2s, rsem.at[1])


def settle(*refs):
    count = len(refs) // 2
    sems = refs[-1]
    copies = [pltpu.make_async_copy(refs[i], refs[count + i], sems.at[i]) for i in range(count)]
    for copy in copies:
        copy.start()
    for copy in copies:
        copy.wait()


def body(
    loader_rows, load_owner, load_slot, valid_frames, next_owner, pixel_cache, act_cache, res_cache,
    stem_weight, norm_gain, norm_bias, conv_weight, down_weight,
):
    vm = pl.BlockSpec(memory_space=pltpu.VMEM)
    sm = pl.BlockSpec(memory_space=pltpu.SMEM)
    hbm = pl.BlockSpec(memory_space=pl.ANY)
    dma = pltpu.SemaphoreType.DMA
    shapes = ((4, 8, 8, C2), (32, 48), (N, 8, 128), (N, 8, 128))
    parts = pl.pallas_call(
        kernel,
        out_shape=tuple(pltpu.VMEM(s, BF16) for s in shapes),
        in_specs=[sm, sm] + [hbm] * 13,
        out_specs=(vm, vm, vm, vm),
        scratch_shapes=[
            pltpu.VMEM((48, 128), BF16),
            pltpu.VMEM((1, 128), I32),
            pltpu.VMEM((1, 128), I32),
            pltpu.VMEM((32, 48), BF16),
            pltpu.VMEM((27, 3, 128), BF16),
            pltpu.VMEM((1, 128), F32),
            pltpu.VMEM((1, 128), F32),
            pltpu.VMEM((2, 16, W, 128), BF16),
            pltpu.VMEM((2, 16, W, 128), BF16),
            pltpu.VMEM((1152, 256), BF16),
            pltpu.VMEM((1152, 128), BF16),
            pltpu.VMEM((3456, C2), BF16),
            pltpu.VMEM((128, 256), BF16),
            pltpu.VMEM((N, 2, 128), F32),
            pltpu.VMEM((N, 2, 128), F32),
            pltpu.VMEM((N, 2, 128), F32),
            pltpu.VMEM((N, 2, 128), F32),
            pltpu.VMEM((256, 128), F32),
            pltpu.VMEM((22, 16, 128), BF16),
            pltpu.VMEM((22, 16, 128), BF16),
            pltpu.VMEM((27, 8, 128), F32),
            pltpu.VMEM((512, 2048), BF16),
            pltpu.VMEM((NY, 8, W, 128), F32),
            pltpu.VMEM((NY, 8, W, 128), F32),
            pltpu.VMEM((16, 128), F32),
            pltpu.VMEM((3, 16, 128), F32),
            pltpu.VMEM((16, 128), F32),
            pltpu.VMEM((3, 16, 128), F32),
            pltpu.VMEM((NY, 10, W, 384), BF16),
            pltpu.VMEM((NY, 4, W, 384), BF16),
            pltpu.VMEM((NY, 2, W, 128), F32),
            pltpu.VMEM((9, 2, 2, 5, 8, 384), F32),
            pltpu.VMEM((17, 10, W, 128), F32),
            pltpu.VMEM((2, 3, W, 128), BF16),
            pltpu.VMEM((2, 1, W, 128), BF16),
            pltpu.VMEM((2, 6, 8, 128), BF16),
            pltpu.VMEM((N, 8, 128), BF16),
            pltpu.VMEM((N, 8, 128), BF16),
            pltpu.VMEM((N, 8, 128), BF16),
            pltpu.VMEM((N, 8, 128), BF16),
            pltpu.VMEM((N, 8, 128), BF16),
            pltpu.VMEM((N, 8, 128), BF16),
            pltpu.VMEM((N, 8, 128), BF16),
            pltpu.VMEM((N, 8, 128), BF16),
            pltpu.VMEM((512, 512), BF16),
            dma((21,)),
            dma((2,)),
            dma((2,)),
            dma((2, 6)),
            dma((2, 4)),
            dma((2, 2)),
            dma((2, 2)),
            dma((2, 3)),
            dma((2, 3)),
            dma((2, 2)),
            dma((2, 2)),
        ],
        compiler_params=pltpu.CompilerParams(
            collective_id=0, has_side_effects=True, vmem_limit_bytes=60 * 1024 * 1024
        ),
        name="encoder",
    )(
        valid_frames, next_owner, loader_rows[0].T, load_owner, load_slot,
        pixel_cache.reshape(32, 48), stem_weight.reshape(27, 3, 128), norm_gain[None], norm_bias[None],
        act_cache[0], res_cache[0], act_cache.reshape(N, 8, 128), res_cache.reshape(N, 8, 128),
        conv_weight.reshape(9, 384, C1), down_weight.reshape(3456, C2),
    )
    lat, pix, act, res = pl.pallas_call(
        settle,
        out_shape=tuple(jax.ShapeDtypeStruct(s, BF16) for s in shapes),
        in_specs=[hbm] * 4,
        out_specs=(hbm,) * 4,
        scratch_shapes=[dma((4,))],
        name="settle",
    )(*[pltpu.with_memory_space_constraint(p, pltpu.VMEM) for p in parts])
    return (
        lat[None],
        pix.reshape(1, 2, 16, 48),
        act.reshape(1, 2, 16, 16, 128),
        res.reshape(1, 2, 16, 16, 128),
    )


def solution(mesh):
    in_specs = (
        P("stream", "strip", None),
        P("stream", "strip"),
        P("stream", "strip"),
        P("stream"),
        P("stream"),
        P("stream", None, "strip", None),
        P("stream", None, "strip", None, None),
        P("stream", None, "strip", None, None),
        P(),
        P(),
        P(),
        P(),
        P(),
    )
    out_specs = (
        P("stream", None, "strip", None, None),
        P("stream", None, "strip", None),
        P("stream", None, "strip", None, None),
        P("stream", None, "strip", None, None),
    )
    return jax.shard_map(body, mesh=mesh, in_specs=in_specs, out_specs=out_specs, check_vma=False)
```

```python
import functools

import jax
import jax.numpy as jnp
from jax import lax
from jax.experimental import pallas as pl
from jax.experimental.pallas import tpu as pltpu
from jax.sharding import PartitionSpec as P

F32 = jnp.float32
BF16 = jnp.bfloat16
I32 = jnp.int32
MESH = pl.DeviceIdType.MESH
EPS = 1e-06

T = 8
YS = 16
NY = 20
W = 16
C1 = 128
C2 = 256
N = 64

OFFSETS = sorted(
    [(dy, dz, dx, dc) for dy in range(4) for dz in range(2) for dx in range(4) for dc in range(2)][1:],
    key=lambda o: -(min(o[0], 4 - o[0]) + o[1] + min(o[2], 4 - o[2])),
)


def dot(a, b):
    return lax.dot_general(a, b, (((1,), (0,)), ((), ())), preferred_element_type=F32)


def iota(shape, dim):
    return lax.broadcasted_iota(I32, shape, dim)


def onehot(mask):
    return jnp.where(mask, 1.0, 0.0).astype(BF16)


def group_sum(x):
    lane = iota(x.shape, 1)
    size = x.shape[1]
    x = x + jnp.where(lane % 2 == 0, pltpu.roll(x, size - 1, 1), pltpu.roll(x, 1, 1))
    return x + jnp.where(lane % 4 < 2, pltpu.roll(x, size - 2, 1), pltpu.roll(x, 2, 1))


def shifted(x, by):
    col = iota(x.shape, 1)
    rolled = pltpu.roll(x, by % W, 1)
    return jnp.where(col == (0 if by == 1 else W - 1), 0.0, rolled)


def kernel(
    v_ref, nown_ref, *refs,
):
    fetched, rest = refs[:13], refs[13:]
    work(v_ref, nown_ref, fetched, *rest)


def work(
    v_ref, nown_ref, fetched,
    lat_ref, pixo_ref, acto_ref, reso_ref,
    rows_ref, owner_ref, slot_ref, pixc_ref, sw_ref, gain_ref, bias_ref, actc_ref, resc_ref, cw01, cw2, dw,
    rx, lsend, lrecv, fsend, frecv, vmat, ph, fph, wpad, bmat, stem, fstem, stat_s, stat_r, fstat_s, fstat_r,
    act, fact, fcache, dmat, rown, hact, hres, fhact,
    a1s, a1r, a2s, a2r, r1s, r1r, r2s, r2r, perm,
    wsem, lsem, fsem, hsem, gsem, xsem, ysem, tsem, usem, asem, rsem,
):
    me = lax.axis_index("stream")
    strip = lax.axis_index("strip")
    pc, px, pz, py = lax.rem(me, 2), lax.rem(me // 2, 4), lax.rem(me // 8, 2), me // 16
    ids_y = [lax.rem(py + d, 4) * 16 for d in range(4)]
    ids_z = [lax.rem(pz + d, 2) * 8 for d in range(2)]
    ids_x = [lax.rem(px + d, 4) * 2 for d in range(4)]
    ids_c = [lax.rem(pc + d, 2) for d in range(2)]
    peers = [ids_y[o[0]] + ids_z[o[1]] + ids_x[o[2]] + ids_c[o[3]] for o in OFFSETS]
    up = lax.rem(strip + 3, 4)
    down = lax.rem(strip + 1, 4)

    bar = pltpu.get_barrier_semaphore()
    for p in peers:
        pl.semaphore_signal(bar, inc=1, device_id={"stream": p}, device_id_type=MESH)
    for d in range(1, 4):
        pl.semaphore_signal(bar, inc=1, device_id={"strip": lax.rem(strip + d, 4)}, device_id_type=MESH)
    homes = (
        rows_ref, owner_ref, slot_ref, pixc_ref, sw_ref, gain_ref, bias_ref, actc_ref, resc_ref, a1s, r1s
    )
    loads = [pltpu.make_async_copy(fetched[i], homes[i], wsem.at[i]) for i in range(11)]
    weights = [pltpu.make_async_copy(fetched[12], dw, wsem.at[11])]
    for a in range(3):
        rows = pl.ds(a * 384, 384)
        for b in range(3):
            home = cw2.at[rows] if b == 2 else cw01.at[rows, pl.ds(b * 128, 128)]
            weights.append(pltpu.make_async_copy(fetched[11].at[3 * a + b], home, wsem.at[12 + 3 * a + b]))
    for copy in loads + weights:
        copy.start()
    for copy in loads:
        copy.wait()
    v = jnp.clip(v_ref[0], 1, T)

    rx[...] = jnp.zeros((128, 256), BF16)
    rx[0:48, 0:128] = rows_ref[...]
    rx[48:96, 128:256] = rows_ref[...]
    owner = owner_ref[...]
    named = jnp.where(owner == iota((N, 128), 0), 1.0, 0.0)
    ahead = onehot(iota((128, 128), 0) < iota((128, 128), 1))
    count = dot(named.astype(BF16), ahead)
    pick0 = jnp.where(count < 0.5, named, 0.0)
    pick1 = named - pick0
    picks = jnp.concatenate([pick0, pick1], axis=1).astype(BF16)
    send = lax.dot_general(picks, rx[...], (((1,), (1,)), ((), ())), preferred_element_type=F32)
    slot = slot_ref[...].astype(F32)
    slot0 = jnp.sum(pick0 * slot, axis=1, keepdims=True)
    slot1 = jnp.sum(pick1 * slot, axis=1, keepdims=True)
    lane = iota((N, 128), 1)
    send = jnp.where(lane == 96, slot0, send)
    send = jnp.where(lane == 97, slot1, send)
    send = jnp.where(lane == 98, nown_ref[0].astype(F32), send)
    send = jnp.where(lane == 99, v.astype(F32), send)
    vmat[...] = jnp.zeros((256, 128), F32)
    vmat[128:160, 0:48] = pixc_ref[...].astype(F32)
    lsend[:, 0:1, :] = send.reshape(N, 1, 128)
    lsend[:, 1:2, :] = vmat[128:192].reshape(N, 1, 128)

    wpad[...] = jnp.zeros(wpad.shape, F32)
    wpad[:, 0:3, :] = sw_ref[...].astype(F32)
    wp = wpad[...].reshape(9, 24, 128).astype(BF16)
    wide = jnp.concatenate([wp[i] for i in range(9)], axis=1)
    bw, bc, bk = iota((16, 3, 16, 24), 0), iota((16, 3, 16, 24), 1), iota((16, 3, 16, 24), 2)
    bl = iota((16, 3, 16, 24), 3)
    band = onehot((bl % 8 == bc) & (bk == bw + bl // 8 - 1)).reshape(768, 24)
    banded = dot(band, wide).astype(BF16)
    bmat[432:512, :] = jnp.zeros((80, 2048), BF16)
    for w in range(W):
        for tap in range(9):
            bmat[tap * 48 : tap * 48 + 48, w * 128 : w * 128 + 128] = banded[
                w * 48 : w * 48 + 48, tap * 128 : tap * 128 + 128
            ]
    ph[21:22] = jnp.zeros((1, 16, 128), BF16)
    fph[21:22] = jnp.zeros((1, 16, 128), BF16)
    fcache[19:20] = jnp.zeros((1, 2, W, 128), F32)

    def three(value):
        return jnp.concatenate([shifted(value, 1), value, shifted(value, -1)], axis=2).astype(BF16)

    for f in range(2):
        act[2:18, f] = three(actc_ref[f].astype(F32))

    pl.semaphore_wait(bar, N - 1 + 3)

    def exchange(src, dst, sems):
        for p in peers:
            pltpu.make_async_remote_copy(
                src_ref=src.at[p], dst_ref=dst.at[me], send_sem=sems.at[0], recv_sem=sems.at[1],
                device_id={"stream": p}, device_id_type=MESH,
            ).start()
        pltpu.make_async_copy(src.at[me], dst.at[me], sems.at[1]).start()

    def arrived(dst, sems):
        pltpu.make_async_copy(dst, dst, sems.at[1]).wait()

    def drained(src, sems):
        part = src.at[pl.ds(0, N - 1)]
        pltpu.make_async_copy(part, part, sems.at[0]).wait()

    def to_strip(src, dst, other, sems, i):
        copy = pltpu.make_async_remote_copy(
            src_ref=src, dst_ref=dst, send_sem=sems.at[0, i], recv_sem=sems.at[1, i],
            device_id={"strip": other}, device_id_type=MESH,
        )
        copy.start()
        return copy

    exchange(lsend, lrecv, lsem)
    exchange(a1s, a1r, asem.at[0])
    exchange(r1s, r1r, rsem.at[0])
    halo = []
    for f in range(2):
        halo.append(to_strip(actc_ref.at[f, pl.ds(14, 2)], hact.at[f, pl.ds(0, 2)], down, hsem, 3 * f))
        halo.append(to_strip(actc_ref.at[f, pl.ds(0, 1)], hact.at[f, pl.ds(2, 1)], up, hsem, 3 * f + 1))
        halo.append(to_strip(resc_ref.at[f, pl.ds(15, 1)], hres.at[f], down, hsem, 3 * f + 2))

    col = iota((N, 128), 1)
    row = iota((N, 128), 0)

    def assemble(got, place, place_c):
        vmat[0:64, :] = jnp.where(col < 48, got, 0.0)
        vmat[64:128, :] = jnp.where(col < 48, pltpu.roll(got, 80, 1), 0.0)
        put = onehot(iota((256, 256), 0) == jnp.concatenate([place, place_c], axis=1))
        return dot(put, vmat[...].astype(BF16)).astype(BF16)

    def slots_of(got):
        diag = jnp.where(col == row, got[:, 96:97], 0.0) + jnp.where(col == row + N, got[:, 97:98], 0.0)
        return jnp.sum(diag, axis=0, keepdims=True).astype(I32)

    def rims(pixels, sems):
        return [
            to_strip(pixels.at[pl.ds(16, 3)], pixels.at[pl.ds(0, 3)], down, sems, 0),
            to_strip(pixels.at[pl.ds(3, 2)], pixels.at[pl.ds(19, 2)], up, sems, 1),
        ]

    def stem_of(pixels, out, sums):
        pf = pixels[...].astype(F32)
        yy = iota((22, 16, 128), 0)
        live = ((yy >= 3) | (strip > 0)) & ((yy < 19) | (strip < 3))
        pf = jnp.where(live, pf, 0.0)
        ll = iota((NY * 8, 128), 1)
        parts = [jnp.zeros((NY * 8, 128), F32) for _ in range(4)]
        for a in range(3):
            xa = pf[:, a : a + 8, :]
            for b in range(3):
                x = xa[b : b + NY].reshape(NY * 8, 128)
                off = 48 * (3 * a + b)
                q, r = off // 128, off % 128
                if r:
                    x = pltpu.roll(x, r, 1)
                if r + 48 > 128:
                    parts[q] = parts[q] + jnp.where(ll >= r, x, 0.0)
                    parts[q + 1] = parts[q + 1] + jnp.where(ll < r, x, 0.0)
                else:
                    parts[q] = parts[q] + x
        lhs = jnp.concatenate(parts, axis=1).astype(BF16)
        flat = out.reshape(NY * 8 * W, 128)
        s1 = jnp.zeros((8, 128), F32)
        s2 = jnp.zeros((8, 128), F32)
        for w in range(0, W, 2):
            pair = dot(lhs, bmat[:, w * 128 : w * 128 + 256]).astype(BF16).astype(F32)
            for h in range(2):
                block = pair[:, h * 128 : h * 128 + 128]
                flat[pl.ds(w + h, NY * 8, stride=W), :] = block
                own = block.reshape(NY, 8, 128)[2:18]
                s1 = s1 + jnp.sum(own, axis=0)
                s2 = s2 + jnp.sum(own * own, axis=0)
        sums[0:8] = s1
        sums[8:16] = s2

    def share(sums, others, sems):
        return [to_strip(sums, others.at[d - 1], lax.rem(strip + d, 4), sems, d - 1) for d in range(1, 4)]

    def scale_of(sums, others):
        both = sums[...] + others[0] + others[1] + others[2]
        both = group_sum(both) * (1.0 / (64 * 16 * 4))
        mean = both[0:8]
        inv = lax.rsqrt(both[8:16] - mean * mean + EPS)
        gain = inv * gain_ref[...]
        bias = bias_ref[...] - mean * gain
        return gain.reshape(8, 1, 128), bias.reshape(8, 1, 128)

    def silu_row(y, x, gain, bias):
        u = x * gain + bias
        u = u / (1.0 + jnp.exp(-u))
        return jnp.where(((y >= 2) | (strip > 0)) & ((y < 18) | (strip < 3)), u, 0.0)

    arrived(lrecv, lsem)
    got = lrecv[:, 0:1, :].reshape(N, 128)
    tgt = got[:, 98:99]
    tgt1 = jnp.sum(jnp.where(col == row, tgt, 0.0), axis=0, keepdims=True).astype(I32)
    perm1 = onehot((row == tgt1) & (col < N))
    blank = jnp.zeros((N, 128), F32)
    mine = jnp.concatenate([lsend[:, 0:1, :].reshape(N, 128), blank], axis=0).astype(BF16)
    theirs = jnp.concatenate([lrecv[:, 1:2, :].reshape(N, 128), blank], axis=0).astype(BF16)
    fsend[:, 0:1, :] = dot(perm1, mine).reshape(N, 1, 128)
    fsend[:, 1:2, :] = dot(perm1, theirs).reshape(N, 1, 128)
    exchange(fsend, frecv, fsem)
    fv = jnp.sum(jnp.where(tgt == me.astype(F32), got[:, 99:100] + jnp.zeros((N, 128), F32), 0.0), axis=0, keepdims=True)
    fv = fv.astype(I32)

    slots = slots_of(got)
    k2 = iota((1, 128), 1)
    pix = assemble(got, (slots % 16) * 16 + slots // 16 + 2, jnp.where(k2 < 32, (k2 % 16) * 16 + k2 // 16, -1))
    ph[3:19] = pix.reshape(16, 16, 128)
    pix_rims = rims(ph, xsem)

    k = iota((N, 512), 1)
    spread = jnp.where(k // 8 == iota((N, 512), 0), tgt * 8.0 + (k % 8).astype(F32), 0.0)
    tgt8 = jnp.sum(spread, axis=0, keepdims=True).astype(I32)
    perm[...] = onehot(iota((512, 512), 0) == tgt8)

    def onward(src, out):
        flat = src[...].astype(F32).reshape(512, 128).astype(BF16)
        out[...] = dot(perm[...], flat).reshape(N, 8, 128).astype(BF16)

    for copy in pix_rims:
        copy.wait()
    stem_of(ph, stem, stat_s)
    stats = share(stat_s, stat_r, tsem)
    arrived(a1r, asem.at[0])
    onward(a1r, a2s)
    exchange(a2s, a2r, asem.at[1])

    arrived(frecv, fsem)
    fgot = frecv[:, 0:1, :].reshape(N, 128)
    vmat[128:160] = frecv[:, 1:2, :].reshape(N, 128)[0:32]
    slots = slots_of(fgot)
    frame = slots // 16 + 6 - fv
    frame_c = k2 // 16 + 4 - fv
    place = jnp.where((frame >= 0) & (frame < 6), (slots % 16) * 16 + frame, -1)
    place_c = jnp.where((frame_c >= 0) & (k2 < 32), (k2 % 16) * 16 + frame_c, -1)
    fpix = assemble(fgot, place, place_c)
    fph[3:19] = fpix.reshape(16, 16, 128)
    fpix_rims = rims(fph, ysem)
    pi, pq = iota((N, 256), 0), iota((N, 256), 1)
    sel = onehot(pq == (pi % 16) * 16 + 4 + pi // 16)
    pixo_ref[...] = dot(sel, fpix)[0:32, 0:48].astype(BF16)
    arrived(r1r, rsem.at[0])
    onward(r1r, r2s)
    exchange(r2s, r2r, rsem.at[1])

    for copy in weights:
        copy.wait()
    for copy in halo:
        copy.wait()
    for f in range(2):
        ha = hact[f].astype(F32)
        act[0:2, f] = three(jnp.where(strip > 0, ha[0:2], 0.0))
        act[18:19, f] = three(jnp.where(strip < 3, ha[2:3], 0.0))
        rown[1:17, f] = resc_ref[f].astype(F32)
        rown[0:1, f] = jnp.where(strip > 0, hres[f].astype(F32), 0.0)

    for copy in stats:
        copy.wait()
    gain, bias = scale_of(stat_s, stat_r)

    def act_row(y, carry):
        act[y, 2:10] = three(silu_row(y, stem[y], gain, bias))
        return carry

    lax.fori_loop(0, NY, act_row, 0, unroll=4)

    for copy in fpix_rims:
        copy.wait()
    stem_of(fph, fstem, fstat_s)
    fstats = share(fstat_s, fstat_r, usem)

    arrived(a2r, asem.at[1])
    fhalo = []
    for f in range(2):
        fhalo.append(to_strip(a2r.at[pl.ds(f * 32 + 28, 4)], fhact.at[f, pl.ds(0, 4)], down, gsem, 2 * f))
        fhalo.append(to_strip(a2r.at[pl.ds(f * 32, 2)], fhact.at[f, pl.ds(4, 2)], up, gsem, 2 * f + 1))
        fcache[2:18, f] = a2r[f * 32 : f * 32 + 32].astype(F32).reshape(16, W, 128)

    def conv(x, first, count, frames):
        def lhs(y, n):
            return jnp.concatenate([x(y, n, a).reshape(n * frames * W, 384) for a in range(3)], axis=1)

        pair = dot(lhs(first, count + 1), cw01[...]).reshape(count + 1, frames, W, 256)
        last = dot(lhs(first + 2, count), cw2[...]).reshape(count, frames, W, 128)
        return pair[:count, :, :, :128] + pair[1:, :, :, 128:] + last

    def taps(ref_slice):
        return jnp.concatenate([ref_slice(a, b) for a in range(3) for b in range(3)], axis=1)

    keep = (iota((17, 4, W, 128), 0) > 0) | (strip > 0)

    def half(h):
        def rows(y, n, a):
            return act[y : y + n, a + 4 * h : 4 + a + 4 * h]

        res = conv(rows, 0, 17, 4)
        res = (res + stem[1:18, 4 * h : 4 * h + 4]).astype(BF16).astype(F32)
        rown[:, 2 + 4 * h : 6 + 4 * h] = jnp.where(keep, res, 0.0)

    half(0)
    half(1)

    for copy in fhalo:
        copy.wait()
    for f in range(2):
        ha = fhact[f].astype(F32).reshape(3, W, 128)
        fcache[0:2, f] = jnp.where(strip > 0, ha[0:2], 0.0)
        fcache[18:19, f] = jnp.where(strip < 3, ha[2:3], 0.0)
    for copy in fstats:
        copy.wait()
    fgain, fbias = scale_of(fstat_s, fstat_r)

    def fact_row(y, carry):
        u = silu_row(y, fstem[y, 0:4], fgain[0:4], fbias[0:4])
        c = fcache[y]
        u0 = jnp.where(fv == 2, c[0], jnp.where(fv == 3, c[1], u[0]))
        u1 = jnp.where(fv == 1, c[0], jnp.where(fv == 2, c[1], u[1]))
        u2 = jnp.where(fv == 1, c[1], u[2])
        fact[y] = three(jnp.stack([u0, u1, u2, u[3]]))
        return carry

    lax.fori_loop(1, NY - 1, fact_row, 0, unroll=6)

    for f in range(2):
        acto_ref[f * 32 : f * 32 + 32] = (
            fact[2:18, 2 + f, :, 128:256].astype(F32).reshape(32, 8, 128).astype(BF16)
        )

    def next_rows(y, n, a):
        return fact[y : y + n, a : a + 2]

    arrived(r2r, rsem.at[1])
    extra = conv(next_rows, 1, 16, 2)
    for f in range(2):
        new = (extra[:, f] + fstem[2:18, 2 + f]).astype(BF16).astype(F32)
        if f == 0:
            new = jnp.where(fv == 1, r2r[32:64].astype(F32).reshape(16, W, 128), new)
        reso_ref[f * 32 : f * 32 + 32] = new.reshape(32, 8, 128).astype(BF16)

    flat = rown.reshape(17 * 10 * W, 128)
    even = flat[pl.ds(0, 17 * 10 * 8, stride=2), :].reshape(170, 8, 128)
    odd = flat[pl.ds(1, 17 * 10 * 8, stride=2), :].reshape(170, 8, 128)
    before = jnp.where(iota((170, 8, 128), 1) == 0, 0.0, pltpu.roll(odd, 1, 1))
    full = jnp.concatenate([before, even, odd], axis=2).reshape(17, 10, 8, 384)
    for y in range(17):
        for f in range(10):
            dmat[y // 2, y % 2, f % 2, f // 2] = full[y, f]

    def down_taps(a, b):
        return dmat[b // 2 : b // 2 + 8, b % 2, a % 2, a // 2 : a // 2 + 4].reshape(256, 384).astype(BF16)

    lat = dot(taps(down_taps), dw[...]).reshape(8, 4, 8, 256)
    for t in range(4):
        lat_ref[t] = jnp.where(2 * t < v, lat[:, t], 0.0).astype(BF16)

    drained(lsend, lsem)
    drained(fsend, fsem)
    drained(a1s, asem.at[0])
    drained(r1s, rsem.at[0])
    drained(a2s, asem.at[1])
    drained(r2s, rsem.at[1])


def settle(*refs):
    count = len(refs) // 2
    sems = refs[-1]
    copies = [pltpu.make_async_copy(refs[i], refs[count + i], sems.at[i]) for i in range(count)]
    for copy in copies:
        copy.start()
    for copy in copies:
        copy.wait()


def body(
    loader_rows, load_owner, load_slot, valid_frames, next_owner, pixel_cache, act_cache, res_cache,
    stem_weight, norm_gain, norm_bias, conv_weight, down_weight,
):
    vm = pl.BlockSpec(memory_space=pltpu.VMEM)
    sm = pl.BlockSpec(memory_space=pltpu.SMEM)
    hbm = pl.BlockSpec(memory_space=pl.ANY)
    dma = pltpu.SemaphoreType.DMA
    shapes = ((4, 8, 8, C2), (32, 48), (N, 8, 128), (N, 8, 128))
    parts = pl.pallas_call(
        kernel,
        out_shape=tuple(pltpu.VMEM(s, BF16) for s in shapes),
        in_specs=[sm, sm] + [hbm] * 13,
        out_specs=(vm, vm, vm, vm),
        scratch_shapes=[
            pltpu.VMEM((48, 128), BF16),
            pltpu.VMEM((1, 128), I32),
            pltpu.VMEM((1, 128), I32),
            pltpu.VMEM((32, 48), BF16),
            pltpu.VMEM((27, 3, 128), BF16),
            pltpu.VMEM((1, 128), F32),
            pltpu.VMEM((1, 128), F32),
            pltpu.VMEM((2, 16, W, 128), BF16),
            pltpu.VMEM((2, 16, W, 128), BF16),
            pltpu.VMEM((1152, 256), BF16),
            pltpu.VMEM((1152, 128), BF16),
            pltpu.VMEM((3456, C2), BF16),
            pltpu.VMEM((128, 256), BF16),
            pltpu.VMEM((N, 2, 128), F32),
            pltpu.VMEM((N, 2, 128), F32),
            pltpu.VMEM((N, 2, 128), F32),
            pltpu.VMEM((N, 2, 128), F32),
            pltpu.VMEM((256, 128), F32),
            pltpu.VMEM((22, 16, 128), BF16),
            pltpu.VMEM((22, 16, 128), BF16),
            pltpu.VMEM((27, 8, 128), F32),
            pltpu.VMEM((512, 2048), BF16),
            pltpu.VMEM((NY, 8, W, 128), F32),
            pltpu.VMEM((NY, 8, W, 128), F32),
            pltpu.VMEM((16, 128), F32),
            pltpu.VMEM((3, 16, 128), F32),
            pltpu.VMEM((16, 128), F32),
            pltpu.VMEM((3, 16, 128), F32),
            pltpu.VMEM((NY, 10, W, 384), BF16),
            pltpu.VMEM((NY, 4, W, 384), BF16),
            pltpu.VMEM((NY, 2, W, 128), F32),
            pltpu.VMEM((9, 2, 2, 5, 8, 384), F32),
            pltpu.VMEM((17, 10, W, 128), F32),
            pltpu.VMEM((2, 3, W, 128), BF16),
            pltpu.VMEM((2, 1, W, 128), BF16),
            pltpu.VMEM((2, 6, 8, 128), BF16),
            pltpu.VMEM((N, 8, 128), BF16),
            pltpu.VMEM((N, 8, 128), BF16),
            pltpu.VMEM((N, 8, 128), BF16),
            pltpu.VMEM((N, 8, 128), BF16),
            pltpu.VMEM((N, 8, 128), BF16),
            pltpu.VMEM((N, 8, 128), BF16),
            pltpu.VMEM((N, 8, 128), BF16),
            pltpu.VMEM((N, 8, 128), BF16),
            pltpu.VMEM((512, 512), BF16),
            dma((21,)),
            dma((2,)),
            dma((2,)),
            dma((2, 6)),
            dma((2, 4)),
            dma((2, 2)),
            dma((2, 2)),
            dma((2, 3)),
            dma((2, 3)),
            dma((2, 2)),
            dma((2, 2)),
        ],
        compiler_params=pltpu.CompilerParams(
            collective_id=0, has_side_effects=True, vmem_limit_bytes=60 * 1024 * 1024
        ),
        name="encoder",
    )(
        valid_frames, next_owner, loader_rows[0].T, load_owner, load_slot,
        pixel_cache.reshape(32, 48), stem_weight.reshape(27, 3, 128), norm_gain[None], norm_bias[None],
        act_cache[0], res_cache[0], act_cache.reshape(N, 8, 128), res_cache.reshape(N, 8, 128),
        conv_weight.reshape(9, 384, C1), down_weight.reshape(3456, C2),
    )
    lat, pix, act, res = pl.pallas_call(
        settle,
        out_shape=tuple(jax.ShapeDtypeStruct(s, BF16) for s in shapes),
        in_specs=[hbm] * 4,
        out_specs=(hbm,) * 4,
        scratch_shapes=[dma((4,))],
        name="settle",
    )(*[pltpu.with_memory_space_constraint(p, pltpu.VMEM) for p in parts])
    return (
        lat[None],
        pix.reshape(1, 2, 16, 48),
        act.reshape(1, 2, 16, 16, 128),
        res.reshape(1, 2, 16, 16, 128),
    )


def solution(mesh):
    in_specs = (
        P("stream", "strip", None),
        P("stream", "strip"),
        P("stream", "strip"),
        P("stream"),
        P("stream"),
        P("stream", None, "strip", None),
        P("stream", None, "strip", None, None),
        P("stream", None, "strip", None, None),
        P(),
        P(),
        P(),
        P(),
        P(),
    )
    out_specs = (
        P("stream", None, "strip", None, None),
        P("stream", None, "strip", None),
        P("stream", None, "strip", None, None),
        P("stream", None, "strip", None, None),
    )
    return jax.shard_map(body, mesh=mesh, in_specs=in_specs, out_specs=out_specs, check_vma=False)
```
